512 devices in a mesh: gx: 32 (over x, y), gy: 8 (over z_lo, core), gz: 2 (over z_hi).
Axes of the slice: x: 4, y: 8, z: 8 (z_hi: 2, z_lo: 4; z = z_hi * 4 + z_lo), core: 2. Of those that a mesh axis runs over, the one named last changes fastest.
Arguments:
- populations: float32 [19, 128, 32, 2048], P(None, 'gx', 'gz', 'gy'), may hold values from 0.01 to 0.21
- nozzle_mask: int32 [128, 2048], P('gx', 'gy'), may hold values 0 or 1
- wall_type: int32 [128, 2048], P('gx', 'gy'), may hold values from 0 to 1
- solid_temp: float32 [128, 64, 2048], P('gx', None, ('gy', 'gz')), may hold values from -6 to 6
- diffusion: float32 [128, 64, 2048], P('gx', None, ('gy', 'gz')), may hold values from 0.3 to 3
- heat_load: float32 [128, 2048], P('gx', ('gy', 'gz')), may hold values from 0.2 to 2
- coolant_temp: float32 [128, 2048], P('gx', ('gy', 'gz')), may hold values from -2 to 0
Outputs:
- populations_next: float32 [19, 128, 32, 2048], P(None, 'gx', 'gz', 'gy')
- solid_next: float32 [128, 64, 2048], P('gx', None, ('gy', 'gz'))
The draws below stay inside these ranges and needn't reach their ends.
Inputs may be any that keep to these rules, and one draw needn't show every extreme that they name: `nozzle_mask`: 1 marks a nozzle opening; it takes precedence over wall_type. `wall_type`: 1 marks an outlet cell of the plate, 0 a closed plate cell.
All inputs are finite; a program needn't handle non-finite values. No bound on the sum of `nozzle_mask` on one device may be relied on, other than what follows from the above.
Results may differ from the reference program's by a relative error of at most 0.0001.
Values sent between devices are 32-bit elements; how exact they have to be, the bound alone decides.
No kernel may reach another device: no remote copies, remote signals or barrier semaphores. Data moves between devices by JAX's collectives and lax.ppermute only.
A program may use at most 64 MiB of HBM per device.

```python
import math
import jax
import jax.numpy as jnp
import numpy as np
from jax import lax

Q = 19
SZ = 64
NX = 128
NY = 2048
NZ = 32


def set_ends(values, key, least, high):
    spot = [jax.random.randint(jax.random.fold_in(key, axis), (), 0, length) for axis, length in enumerate(values.shape)]
    longest = values.shape.index(max(values.shape))
    next_to = spot[:longest] + [(spot[longest] + 1) % values.shape[longest]] + spot[longest + 1:]
    return values.at[tuple(spot)].set(least).at[tuple(next_to)].set(high)


def block_levels(stream_key, dims, shards, smallest, high):
    factor_of = 1.0
    for position, shards_of in shards:
        steps = jax.random.uniform(jax.random.fold_in(jax.random.fold_in(stream_key, 6), position), (shards_of,), jnp.float32, smallest / len(shards), high / len(shards))
        factor_of = factor_of * jnp.repeat(jnp.exp(steps), dims[position] // shards_of).reshape((-1,) + (1,) * (len(dims) - 1 - position))
    return factor_of


def centred(rng, shape, scale, most, pieces=(), held_as=jnp.bfloat16):
    entries = jax.random.normal(rng, shape, jnp.float32) * scale
    if len(pieces) > 0:
        entries = block_levels(rng, shape, pieces, -0.22, 0.18) * entries
    return jnp.clip(entries, min=-most, max=most).astype(held_as)


def setup_inputs(seed: int = 0) -> dict:
    keys = jax.random.split(jax.random.key(seed), 8)
    populations = jnp.clip(0.01 + 0.19999999 * jax.random.uniform(keys[0], (Q, NX, NZ, NY), jnp.float32) ** block_levels(keys[0], (Q, NX, NZ, NY), ((1, 32), (2, 2), (3, 8)), -0.2, 0.2), 0.01, 0.21)
    nozzle_mask = set_ends((jax.random.randint(keys[1], (NX, NY), 0, 4) < 1).astype(jnp.int32), jax.random.fold_in(keys[1], 1), 0, 1)
    wall_type = set_ends(jax.random.randint(keys[2], (NX, NY), 0, 2), jax.random.fold_in(keys[2], 1), 0, 1).astype(jnp.int32)
    solid_temp = centred(keys[3], (NX, SZ, NY), 1.0, 6.0, ((0, 32), (2, 16)), jnp.float32)
    diffusion = jnp.clip(jnp.exp(math.log(3.0) - 2.3025851 * jax.random.uniform(keys[4], (NX, SZ, NY), jnp.float32) ** block_levels(keys[4], (NX, SZ, NY), ((0, 32), (2, 16)), -0.2, 0.2)), 0.3, 3.0)
    heat_load = jnp.clip(jnp.exp(math.log(2.0) - 2.3025851 * jax.random.uniform(keys[5], (NX, NY), jnp.float32) ** block_levels(keys[5], (NX, NY), ((0, 32), (1, 16)), -0.2, 0.2)), 0.2, 2.0)
    coolant_temp = jnp.clip(-2.0 + 2.0 * jax.random.uniform(keys[6], (NX, NY), jnp.float32) ** block_levels(keys[6], (NX, NY), ((0, 32), (1, 16)), -0.2, 0.2), -2.0, 0.0)
    return dict(populations=populations, nozzle_mask=nozzle_mask, wall_type=wall_type, solid_temp=solid_temp, diffusion=diffusion, heat_load=heat_load, coolant_temp=coolant_temp)


JET_SPEED = 0.1
H_BASE = 0.5
H_GAIN = 40.0
SHEAR_RATE = 1.6
ODD_RATE = 1.2
EVEN_RATE = 1.4

def velocity_table():
    return np.array([[0, 0, 0], [1, 0, 0], [-1, 0, 0], [0, 1, 0], [0, -1, 0], [0, 0, 1], [0, 0, -1], [1, 1, 0], [-1, -1, 0], [1, -1, 0], [-1, 1, 0], [1, 0, 1], [-1, 0, -1], [1, 0, -1], [-1, 0, 1], [0, 1, 1], [0, -1, -1], [0, 1, -1], [0, -1, 1]], dtype=np.int32)

def weight_table():
    return np.array([1.0 / 3.0] + [1.0 / 18.0] * 6 + [1.0 / 36.0] * 12, dtype=np.float32)

def opposite_of(member):
    table = velocity_table()
    for other in range(table.shape[0]):
        if np.all(table[other] == -table[member]):
            return other
    return member

def relax_table():
    table = velocity_table().astype(np.float32)
    comp_a = table[:, 0]
    comp_b = table[:, 1]
    comp_c = table[:, 2]
    monomials = [comp_a * 0.0 + 1.0, comp_a, comp_b, comp_c, comp_a * comp_a, comp_b * comp_b, comp_c * comp_c, comp_a * comp_b, comp_b * comp_c, comp_a * comp_c, comp_a * comp_c * comp_c, comp_a * comp_b * comp_b, comp_c * comp_a * comp_a, comp_c * comp_b * comp_b, comp_b * comp_a * comp_a, comp_b * comp_c * comp_c, comp_a * comp_a * comp_c * comp_c, comp_a * comp_a * comp_b * comp_b, comp_c * comp_c * comp_b * comp_b]
    rates = np.array([0.0] * 4 + [SHEAR_RATE] * 6 + [ODD_RATE] * 6 + [EVEN_RATE] * 3, dtype=np.float32)
    ortho = []
    for monomial in monomials:
        vector = monomial.copy()
        for earlier in ortho:
            vector = vector - np.dot(earlier, vector) * earlier
        ortho.append(vector / np.sqrt(np.dot(vector, vector)))
    gram = np.stack(ortho)
    return (gram.T @ (rates[:, None] * gram)).astype(np.float32)

def collide(pops):
    table = jnp.asarray(velocity_table().astype(np.float32))
    weights = jnp.asarray(weight_table())
    density = lax.optimization_barrier(jnp.sum(pops, axis=0))
    momentum = jnp.einsum('qc,qxzy->cxzy', table, pops, precision=lax.Precision.HIGHEST)
    velocity = momentum / density[None]
    project = jnp.einsum('qc,cxzy->qxzy', table, velocity, precision=lax.Precision.HIGHEST)
    square = lax.optimization_barrier(jnp.sum(velocity * velocity, axis=0))
    equil = weights[:, None, None, None] * density[None] * (1.0 + 3.0 * project + 4.5 * project * project - 1.5 * square[None])
    relaxed = jnp.einsum('pq,qxzy->pxzy', jnp.asarray(relax_table()), pops - equil, precision=lax.Precision.HIGHEST)
    return (pops - relaxed, density, velocity)

def wall_coefficient(density_plane, velocity_plane):
    return H_BASE + H_GAIN * lax.optimization_barrier(jnp.sum(velocity_plane * velocity_plane, axis=0))

def apply_walls(moved, post, nozzle, outlet_kind, at_bottom, at_top):
    table = velocity_table()
    weights = weight_table()
    layers = []
    for member in range(table.shape[0]):
        layer = moved[member]
        other = opposite_of(member)
        if table[member, 2] > 0:
            bottom_value = post[other][:, 0, :]
            layer = layer.at[:, 0, :].set(jnp.where(at_bottom, bottom_value, layer[:, 0, :]))
        if table[member, 2] < 0:
            closed_value = post[other][:, -1, :]
            inlet_value = closed_value + 6.0 * float(weights[member]) * JET_SPEED
            outlet_value = post[member][:, -1, :]
            top_value = jnp.where(nozzle == 1, inlet_value, jnp.where(outlet_kind == 1, outlet_value, closed_value))
            layer = layer.at[:, -1, :].set(jnp.where(at_top, top_value, layer[:, -1, :]))
        layers.append(layer)
    return jnp.stack(layers)

def sweep_core(temp, cond, told, load, heat, coolant, neighbours):
    numer = told
    denom = jnp.ones_like(told)
    for near_temp, near_cond in neighbours:
        link = 0.5 * (cond + near_cond)
        numer = numer + link * near_temp
        denom = denom + link
    link = 0.5 * (cond[:, 1:] + cond[:, :-1])
    edge = jnp.zeros_like(cond[:, :1])
    numer = numer + jnp.concatenate([link * temp[:, 1:], edge], axis=1)
    denom = denom + jnp.concatenate([link, edge], axis=1)
    numer = numer + jnp.concatenate([edge, link * temp[:, :-1]], axis=1)
    denom = denom + jnp.concatenate([edge, link], axis=1)
    numer = numer.at[:, 0].add(load)
    numer = numer.at[:, -1].add(heat * coolant)
    denom = denom.at[:, -1].add(heat)
    return numer / denom

def rolled(temp, cond):
    result = []
    for shift_by, axis_id in ((1, 0), (-1, 0), (1, 2), (-1, 2)):
        result.append((jnp.roll(temp, shift_by, axis_id), jnp.roll(cond, shift_by, axis_id)))
    return result

def reference(populations, nozzle_mask, wall_type, solid_temp, diffusion, heat_load, coolant_temp):
    post, density, velocity = collide(populations)
    table = velocity_table()
    moved = jnp.stack([jnp.roll(post[member], (int(table[member, 0]), int(table[member, 2]), int(table[member, 1])), (0, 1, 2)) for member in range(table.shape[0])])
    populations_next = apply_walls(moved, post, nozzle_mask, wall_type, True, True)
    heat = wall_coefficient(density[:, 0, :], velocity[:, :, 0, :])
    first = sweep_core(solid_temp, diffusion, solid_temp, heat_load, heat, coolant_temp, rolled(solid_temp, diffusion))
    solid_next = sweep_core(first, diffusion, solid_temp, heat_load, heat, coolant_temp, rolled(first, diffusion))
    return (populations_next, solid_next)
```

```python
import jax
import jax.numpy as jnp
from jax import lax
from jax.experimental import pallas as pl
from jax.experimental.pallas import tpu as pltpu
from jax.sharding import PartitionSpec as P

F32 = jnp.float32
JET_SPEED = 0.1
H_BASE = 0.5
H_GAIN = 40.0
SHEAR_RATE = 1.6
ODD_RATE = 1.2
EVEN_RATE = 1.4
VEL = (
    (0, 0, 0),
    (1, 0, 0), (-1, 0, 0), (0, 1, 0), (0, -1, 0), (0, 0, 1), (0, 0, -1),
    (1, 1, 0), (-1, -1, 0), (1, -1, 0), (-1, 1, 0),
    (1, 0, 1), (-1, 0, -1), (1, 0, -1), (-1, 0, 1),
    (0, 1, 1), (0, -1, -1), (0, 1, -1), (0, -1, 1),
)
OPP = tuple(VEL.index(tuple(-e for e in v)) for v in VEL)
WEIGHT = (1.0 / 3.0,) + (1.0 / 18.0,) * 6 + (1.0 / 36.0,) * 12
X_UP, X_DN = (1, 7, 9, 11, 13), (2, 10, 8, 14, 12)
Y_UP, Y_DN = (3, 7, 10, 15, 17), (4, 9, 8, 18, 16)
Z_UP, Z_DN = (5, 11, 14, 15, 18), (6, 13, 12, 17, 16)
SX, SZ_, HALF = 4, 16, 128
DEPTH = 64
Z_S, Z_E, Z_ROWS = 40, 56, 64
Y_S, Y_E, Y_D, Y_ROWS = 16, 32, 40, 48
X_U, X_SL, X_SR, X_YP, X_YM, X_R, X_ROWS = 160, 416, 432, 448, 464, 480, 488


def roll(value, shift, axis):
    size = value.shape[axis]
    shift = shift % size
    return value if shift == 0 else pltpu.roll(value, shift, axis)


def lanes(shape):
    return lax.broadcasted_iota(jnp.int32, shape, len(shape) - 1)


def rows_of(shape):
    return lax.broadcasted_iota(jnp.int32, shape, 0)


def collide(f):
    s = {i: f[i] + f[i + 1] for i in range(1, 19, 2)}
    d = {i: f[i] - f[i + 1] for i in range(1, 19, 2)}
    s_ab, s_ac, s_bc = s[7] + s[9], s[11] + s[13], s[15] + s[17]
    rho = (f[0] + s[1]) + (s[3] + s[5]) + (s_ab + s_ac + s_bc)
    m_a = d[1] + (d[7] + d[9]) + (d[11] + d[13])
    m_b = d[3] + (d[7] - d[9]) + (d[15] + d[17])
    m_c = d[5] + (d[11] - d[13]) + (d[15] - d[17])
    inv = 1.0 / rho
    u_a, u_b, u_c = m_a * inv, m_b * inv, m_c * inv
    p_aa, p_bb, p_cc = m_a * u_a, m_b * u_b, m_c * u_c
    p_ab, p_ac, p_bc = m_a * u_b, m_a * u_c, m_b * u_c
    q = p_aa + p_bb + p_cc
    base = rho - 1.5 * q
    t = rho - 2.0 * q
    t_ab = 4.0 * f[0] - 2.0 * (s[1] + s[3]) + s_ab - (t + 0.5 * p_cc)
    t_ac = 4.0 * f[0] - 2.0 * (s[1] + s[5]) + s_ac - (t + 0.5 * p_bb)
    t_bc = 4.0 * f[0] - 2.0 * (s[3] + s[5]) + s_bc - (t + 0.5 * p_aa)
    mean = (2.0 / 7.0) * (t_ab + t_ac + t_bc)
    gain = (SHEAR_RATE - EVEN_RATE) / 12.0
    c_ab, c_ac, c_bc = gain * (t_ab - mean), gain * (t_ac - mean), gain * (t_bc - mean)
    keep, half_keep, half = 1.0 - SHEAR_RATE, 0.5 * (1.0 - SHEAR_RATE), 0.5 * SHEAR_RATE
    odd, pull = 0.5 * (1.0 - ODD_RATE), 3.0 * ODD_RATE
    post = [None] * 19
    post[0] = keep * f[0] + (SHEAR_RATE / 3.0) * base + 4.0 * (c_ab + c_ac + c_bc)

    def put(i, extra, equil, moment, weight):
        even = half_keep * s[i] + equil + extra
        anti = odd * d[i] + (pull * weight) * moment
        post[i] = even + anti
        post[i + 1] = even - anti

    axis = half / 9.0
    for i, p, c, m in ((1, p_aa, c_ab + c_ac, m_a), (3, p_bb, c_ab + c_bc, m_b), (5, p_cc, c_ac + c_bc, m_c)):
        put(i, -2.0 * c, axis * (base + 4.5 * p), m, 1.0 / 18.0)
    diag = half / 18.0
    for i, pp, pq, c, m, n in (
        (7, p_aa + p_bb, p_ab, c_ab, m_a, m_b),
        (11, p_aa + p_cc, p_ac, c_ac, m_a, m_c),
        (15, p_bb + p_cc, p_bc, c_bc, m_b, m_c),
    ):
        even = diag * (base + 4.5 * pp)
        cross = (9.0 * diag) * pq
        put(i, c, even + cross, m + n, 1.0 / 36.0)
        put(i + 2, c, even - cross, m - n, 1.0 / 36.0)
    return post, q * inv


def collide_kernel(pops, temp, cond, load, cool, post, zbuf, yp, ym, xp, xm, own, heat, buf, sems):
    copies = [pltpu.make_async_copy(pops.at[:, x], buf.at[:, x], sems.at[x]) for x in range(SX)]
    for copy in copies:
        copy.start()
    low = lax.axis_index("gz") == 0
    lane = lanes((DEPTH, HALF))
    edges = jnp.zeros((DEPTH, HALF), F32)
    for k, field in enumerate((temp, cond)):
        for x in range(SX):
            at = k * 16 + x * 4
            edges = jnp.where((lane >= at) & (lane < at + 4), roll(field[x], at + 2, 1), edges)
    own[...] = edges
    lane16 = lanes((16, HALF))
    fold = edges[0:16]
    for g in range(1, 4):
        fold = jnp.where(lane16 >= 32 * g, roll(edges[16 * g : 16 * g + 16], 32 * g, 1), fold)
    zbuf[Z_S : Z_S + 16, :] = fold
    for k, field in enumerate((temp, cond)):
        for buffer, near, far in ((xp, 3, 2), (xm, 0, 1)):
            at = X_U + 128 * k
            buffer[at : at + 64, :] = field[near]
            buffer[at + 64 : at + 128, :] = field[far]
    y_up = [jnp.zeros((8, HALF), F32) for _ in range(2)]
    y_dn = [jnp.zeros((8, HALF), F32) for _ in range(2)]
    lane8 = lanes((8, HALF))
    for x in range(SX):
        copies[x].wait()
        for k in range(2):
            z = slice(8 * k, 8 * k + 8)
            for h in range(2):
                y = slice(HALF * h, HALF * h + HALF)
                out, speed = collide([buf[v, x, z, y] for v in range(19)])
                for v in range(19):
                    post[v, x, z, y] = out[v]
                if k == 0:
                    heat[4 * h + x : 4 * h + x + 1, :] = H_BASE + H_GAIN * speed[0:1, :]
                for n in range(5):
                    row = 20 * h + 4 * n + x
                    if k == 0:
                        zbuf[row : row + 1, :] = out[Z_DN[n]][0:1, :]
                    else:
                        down = zbuf[row : row + 1, :]
                        zbuf[row : row + 1, :] = jnp.where(low, out[Z_UP[n]][7:8, :], down)
                    at = 4 * n + x
                    if h == 1:
                        y_up[k] = jnp.where(lane8 == at, roll(out[Y_UP[n]], at - 127, 1), y_up[k])
                    else:
                        y_dn[k] = jnp.where(lane8 == at, roll(out[Y_DN[n]], at, 1), y_dn[k])
                    at = 32 * n + 16 * h + 8 * k
                    if x == 3:
                        xp[at : at + 8, :] = out[X_UP[n]]
                    if x == 0:
                        xm[at : at + 8, :] = out[X_DN[n]]
    for k in range(2):
        yp[8 * k : 8 * k + 8, :] = y_up[k]
        ym[8 * k : 8 * k + 8, :] = y_dn[k]
    lane1 = lanes((1, HALF))
    row = jnp.zeros((1, HALF), F32)
    for k, (field, first) in enumerate(((load, 0), (cool, 0), (heat, 0), (heat, 4))):
        for x in range(SX):
            at = k * 16 + x * 4
            value = field[first + x : first + x + 1, :]
            row = jnp.where((lane1 >= at) & (lane1 < at + 2), roll(value, at + 1, 1), row)
    zbuf[Z_E : Z_E + 4, :] = heat[4:8, :]
    zbuf[Z_E + 4 : Z_E + 5, :] = row
    zbuf[Z_E + 5 : Z_E + 8, :] = jnp.zeros((3, HALF), F32)


def y_kernel(yp, ym, zbuf, zin, outp, outm):
    low = lax.axis_index("gz") == 0
    lane = lanes((1, HALF))
    sent = zin[Z_E + 4 : Z_E + 5, :]
    row = jnp.where((lane >= 32) & low, zbuf[Z_E + 4 : Z_E + 5, :], sent)
    for out, edge, first in ((outp, yp, 20 + 12), (outm, ym, 16)):
        out[0:16, :] = edge[...]
        out[Y_S : Y_S + 16, :] = zin[Z_S : Z_S + 16, :]
        out[Y_E : Y_E + 8, :] = jnp.broadcast_to(row, (8, HALF))
        out[Y_D : Y_D + 4, :] = zin[first : first + 4, :]
        out[Y_D + 4 : Y_D + 8, :] = jnp.zeros((4, HALF), F32)


def x_kernel(inp, inm, zin, ypin, ymin, load, cool, heat, outp, outm, tail, sems):
    low = lax.axis_index("gz") == 0
    left = jnp.where(low, ypin[Y_S : Y_S + 16, :], zin[Z_S : Z_S + 16, :])
    right = jnp.where(low, zin[Z_S : Z_S + 16, :], ymin[Y_S : Y_S + 16, :])
    warm = jnp.where(low, heat[0:4, :], zin[Z_E : Z_E + 4, :])
    copies = []
    for k, (out, x, n) in enumerate(((outp, 3, 1), (outm, 0, 2))):
        part = tail.at[k]
        part[0:16, :] = left
        part[16:32, :] = right
        part[32:48, :] = ypin[0:16, :]
        part[48:64, :] = ymin[0:16, :]
        for h in range(2):
            row = 20 * h + 4 * n + x
            part[64 + h : 65 + h, :] = zin[row : row + 1, :]
        part[66:67, :] = load[x : x + 1, :]
        part[67:68, :] = cool[x : x + 1, :]
        part[68:69, :] = warm[x : x + 1, :]
        part[69:72, :] = jnp.zeros((3, HALF), F32)
        copies.append(pltpu.make_async_copy(part, out.at[X_SL:X_ROWS], sems.at[k]))
    for copy in copies:
        copy.start()
    for copy in copies:
        copy.wait()


def final_kernel(
    post, zin, ypin, ymin, xpin, xmin, nozzle, wall, temp, cond, load, cool, own, heat, zbuf,
    pops_out, solid_out,
):
    low = lax.axis_index("gz") == 0
    lane = lanes((SZ_, HALF))
    layer = rows_of((SZ_, HALF))
    for v, (a, b, c) in enumerate(VEL):
        for x in range(SX):
            s = x - a
            inside = 0 <= s < SX
            edge = xpin if s < 0 else xmin
            if inside:
                tiles = [post[v, s, :, HALF * h : HALF * h + HALF] for h in range(2)]
            else:
                n = (X_UP if s < 0 else X_DN).index(v)
                tiles = [edge[32 * n + 16 * h : 32 * n + 16 * h + 16, :] for h in range(2)]
            beside = None
            if b:
                slab, first = (ypin, X_YP) if b > 0 else (ymin, X_YM)
                k = 4 * (Y_UP if b > 0 else Y_DN).index(v) + (s if inside else (3 if s < 0 else 0))
                to = 0 if b > 0 else HALF - 1
                column = slab[0:16, :] if inside else edge[first : first + 16, :]
                beside = roll(column, to - k, 1)
            if c:
                n = (Z_UP if c > 0 else Z_DN).index(v)
                at = 0 if c > 0 else SZ_ - 1
                for h in range(2):
                    row = zin[20 * h + 4 * n + s : 20 * h + 4 * n + s + 1, :] if inside else edge[X_R + h : X_R + h + 1, :]
                    tiles[h] = jnp.where(layer == at, row, roll(tiles[h], c, 0))
                if b:
                    corner = roll(slab[Y_D + x : Y_D + x + 1, :], b, 1)
                    beside = jnp.where(layer == at, corner, roll(beside, c, 0))
            if b > 0:
                t0, t1 = roll(tiles[0], 1, 1), roll(tiles[1], 1, 1)
                tiles = [jnp.where(lane == 0, beside, t0), jnp.where(lane == 0, t0, t1)]
            elif b < 0:
                t0, t1 = roll(tiles[0], -1, 1), roll(tiles[1], -1, 1)
                tiles = [jnp.where(lane == HALF - 1, t1, t0), jnp.where(lane == HALF - 1, beside, t1)]
            for h in range(2):
                y = slice(HALF * h, HALF * h + HALF)
                if c > 0:
                    back = post[OPP[v], x, 0:1, y]
                    tiles[h] = jnp.where((layer == 0) & low, back, tiles[h])
                elif c < 0:
                    back = post[OPP[v], x, SZ_ - 1 : SZ_, y]
                    through = post[v, x, SZ_ - 1 : SZ_, y]
                    top = jnp.where(
                        nozzle[x : x + 1, y] == 1,
                        back + 6.0 * WEIGHT[v] * JET_SPEED,
                        jnp.where(wall[x : x + 1, y] == 1, through, back),
                    )
                    tiles[h] = jnp.where((layer == SZ_ - 1) & jnp.logical_not(low), top, tiles[h])
                pops_out[v, x, :, y] = tiles[h]

    lane = lanes((DEPTH, HALF))
    depth = rows_of((DEPTH, HALF))
    floor, face = depth == 0, depth == DEPTH - 1

    def spread(folded, at):
        return jnp.concatenate([roll(folded, at - 32 * g, 1) for g in range(4)], axis=0)

    def vertical(c):
        down = jnp.where(face, 0.0, 0.5 * (c + roll(c, -1, 0)))
        return down, roll(down, 1, 0)

    def around(u, links):
        total = None
        for link, near in links:
            total = link * near if total is None else total + link * near
        return total

    U = {x: temp[x] for x in range(SX)}
    C = {x: cond[x] for x in range(SX)}
    for near, far, edge in ((-1, -2, xpin), (4, 5, xmin)):
        U[near], U[far] = edge[X_U : X_U + 64, :], edge[X_U + 64 : X_U + 128, :]
        C[near], C[far] = edge[X_U + 128 : X_U + 192, :], edge[X_U + 192 : X_U + 256, :]
    warm = jnp.where(low, heat[0:4, :], zin[Z_E : Z_E + 4, :])
    loads = {x: load[x : x + 1, :] for x in range(SX)}
    cools = {x: cool[x : x + 1, :] for x in range(SX)}
    warms = {x: warm[x : x + 1, :] for x in range(SX)}
    for x, edge in ((-1, xpin), (4, xmin)):
        loads[x], cools[x], warms[x] = (edge[X_R + 2 + k : X_R + 3 + k, :] for k in range(3))

    left = jnp.where(low, ypin[Y_S : Y_S + 16, :], zin[Z_S : Z_S + 16, :])
    right = jnp.where(low, zin[Z_S : Z_S + 16, :], ymin[Y_S : Y_S + 16, :])
    own_edges = own[...]
    near_first = {}
    side = {}
    row_left = jnp.where(low, ypin[Y_E : Y_E + 1, :], zin[Z_E + 4 : Z_E + 5, :])
    row_right = jnp.where(low, zin[Z_E + 4 : Z_E + 5, :], ymin[Y_E : Y_E + 1, :])
    heat_left = jnp.where(low, roll(row_left, -48, 1), roll(row_left, -32, 1))
    heat_right = jnp.where(low, roll(zbuf[Z_E + 4 : Z_E + 5, :], -49, 1), roll(row_right, -33, 1))
    for name, folded, at, j1, j2, jo, row, h_row, jr in (
        ("left", left, X_SL, 1, 0, 2, row_left, heat_left, 0),
        ("right", right, X_SR, 2, 3, 1, row_right, heat_right, 1),
    ):
        u1, u2 = spread(folded, -j1), spread(folded, -j2)
        c1, c2 = spread(folded, -16 - j1), spread(folded, -16 - j2)
        before, after = xpin[at : at + 16, :], xmin[at : at + 16, :]
        u1 = jnp.where(lane == 124, spread(before, 124 - 12 - j1), jnp.where(lane == 16, spread(after, 16 - j1), u1))
        c1 = jnp.where(lane == 124, spread(before, 124 - 28 - j1), jnp.where(lane == 16, spread(after, -j1), c1))
        side[name] = (u1, c1)
        uo, co = roll(own_edges, -jo, 1), roll(own_edges, -16 - jo, 1)
        g_far, g_own = 0.5 * (c1 + c2), 0.5 * (c1 + co)
        g_up = 0.5 * (c1 + roll(c1, -4, 1))
        g_dn = roll(g_up, 4, 1)
        v_dn, v_up = vertical(c1)
        e_load, e_cool = roll(row, -jr, 1), roll(row, -16 - jr, 1)
        num = u1 + jnp.where(floor, e_load, 0.0) + jnp.where(face, h_row * e_cool, 0.0)
        den = 1.0 + jnp.where(face, h_row, 0.0) + (g_far + g_own) + (g_up + g_dn) + (v_dn + v_up)
        num = num + around(u1, ((g_far, u2), (g_own, uo), (g_up, roll(u1, -4, 1)), (g_dn, roll(u1, 4, 1)),
                                (v_dn, roll(u1, -1, 0)), (v_up, roll(u1, 1, 0))))
        near_first[name] = num / den

    def beside_of(value, left_col, right_col):
        return (
            jnp.where(lane == 0, left_col, roll(value, 1, 1)),
            jnp.where(lane == HALF - 1, right_col, roll(value, -1, 1)),
        )

    def columns(pair, x):
        at = (4 * x) % HALF
        return roll(pair[0], -at, 1), roll(pair[1], HALF - 1 - at, 1)

    pair_u = (side["left"][0], side["right"][0])
    pair_c = (side["left"][1], side["right"][1])
    pair_f = (near_first["left"], near_first["right"])
    g_x = {x: 0.5 * (C[x] + C[x + 1]) for x in range(-2, 5)}
    first, kept = {}, {}
    for x in range(-1, 5):
        c_l, c_r = beside_of(C[x], *columns(pair_c, x))
        u_l, u_r = beside_of(U[x], *columns(pair_u, x))
        g_l, g_r = 0.5 * (C[x] + c_l), 0.5 * (C[x] + c_r)
        v_dn, v_up = vertical(C[x])
        base = U[x] + jnp.where(floor, loads[x], 0.0) + jnp.where(face, warms[x] * cools[x], 0.0)
        den = 1.0 + jnp.where(face, warms[x], 0.0) + (g_x[x - 1] + g_x[x]) + (g_l + g_r) + (v_dn + v_up)
        inv = 1.0 / den
        num = base + around(U[x], ((g_x[x - 1], U[x - 1]), (g_x[x], U[x + 1]), (g_l, u_l), (g_r, u_r),
                                   (v_dn, roll(U[x], -1, 0)), (v_up, roll(U[x], 1, 0))))
        first[x] = num * inv
        kept[x] = (base, inv, g_l, g_r, v_dn, v_up)
    for x in range(SX):
        base, inv, g_l, g_r, v_dn, v_up = kept[x]
        f_l, f_r = beside_of(first[x], *columns(pair_f, x))
        num = base + around(first[x], ((g_x[x - 1], first[x - 1]), (g_x[x], first[x + 1]), (g_l, f_l), (g_r, f_r),
                                       (v_dn, roll(first[x], -1, 0)), (v_up, roll(first[x], 1, 0))))
        solid_out[x] = num * inv


def shape(*dims):
    return jax.ShapeDtypeStruct(dims, F32)


VM = pl.BlockSpec(memory_space=pltpu.VMEM)
ANY = pl.BlockSpec(memory_space=pl.ANY)


def ring(axis, step):
    n = lax.axis_size(axis)
    return [(i, (i + step) % n) for i in range(n)]


def body(populations, nozzle_mask, wall_type, solid_temp, diffusion, heat_load, coolant_temp):
    post, zbuf, yp, ym, xp, xm, own, heat = pl.pallas_call(
        collide_kernel,
        name="collide",
        in_specs=[ANY, VM, VM, VM, VM],
        out_specs=[VM] * 8,
        out_shape=[
            shape(19, SX, SZ_, 2 * HALF), shape(Z_ROWS, HALF), shape(16, HALF), shape(16, HALF),
            shape(X_ROWS, HALF), shape(X_ROWS, HALF), shape(DEPTH, HALF), shape(8, HALF),
        ],
        scratch_shapes=[pltpu.VMEM((19, SX, SZ_, 2 * HALF), F32), pltpu.SemaphoreType.DMA((SX,))],
    )(populations, solid_temp, diffusion, heat_load, coolant_temp)
    zin = lax.ppermute(zbuf, "gz", ring("gz", 1))
    ypo, ymo = pl.pallas_call(
        y_kernel,
        name="pack_y",
        in_specs=[VM] * 4,
        out_specs=[VM] * 2,
        out_shape=[shape(Y_ROWS, HALF)] * 2,
    )(yp, ym, zbuf, zin)
    ypin = lax.ppermute(ypo, "gy", ring("gy", 1))
    ymin = lax.ppermute(ymo, "gy", ring("gy", -1))
    xpo, xmo = pl.pallas_call(
        x_kernel,
        name="pack_x",
        in_specs=[ANY] * 2 + [VM] * 6,
        out_specs=[ANY] * 2,
        out_shape=[shape(X_ROWS, HALF)] * 2,
        scratch_shapes=[pltpu.VMEM((2, X_ROWS - X_SL, HALF), F32), pltpu.SemaphoreType.DMA((2,))],
        input_output_aliases={0: 0, 1: 1},
    )(xp, xm, zin, ypin, ymin, heat_load, coolant_temp, heat)
    xpin = lax.ppermute(xpo, "gx", ring("gx", 1))
    xmin = lax.ppermute(xmo, "gx", ring("gx", -1))
    return pl.pallas_call(
        final_kernel,
        name="finish",
        in_specs=[VM] * 15,
        out_specs=[VM] * 2,
        out_shape=[shape(19, SX, SZ_, 2 * HALF), shape(SX, DEPTH, HALF)],
    )(post, zin, ypin, ymin, xpin, xmin, nozzle_mask, wall_type, solid_temp, diffusion,
      heat_load, coolant_temp, own, heat, zbuf)


def solution(mesh):
    placed = (
        P(None, "gx", "gz", "gy"),
        P("gx", "gy"),
        P("gx", "gy"),
        P("gx", None, ("gy", "gz")),
        P("gx", None, ("gy", "gz")),
        P("gx", ("gy", "gz")),
        P("gx", ("gy", "gz")),
    )
    return jax.shard_map(
        body,
        mesh=mesh,
        in_specs=placed,
        out_specs=(P(None, "gx", "gz", "gy"), P("gx", None, ("gy", "gz"))),
        check_vma=False,
    )
```

```python
import jax
import jax.numpy as jnp
from jax import lax
from jax.experimental import pallas as pl
from jax.experimental.pallas import tpu as pltpu
from jax.sharding import PartitionSpec as P

F32 = jnp.float32
JET_SPEED = 0.1
H_BASE = 0.5
H_GAIN = 40.0
SHEAR_RATE = 1.6
ODD_RATE = 1.2
EVEN_RATE = 1.4
VEL = (
    (0, 0, 0),
    (1, 0, 0), (-1, 0, 0), (0, 1, 0), (0, -1, 0), (0, 0, 1), (0, 0, -1),
    (1, 1, 0), (-1, -1, 0), (1, -1, 0), (-1, 1, 0),
    (1, 0, 1), (-1, 0, -1), (1, 0, -1), (-1, 0, 1),
    (0, 1, 1), (0, -1, -1), (0, 1, -1), (0, -1, 1),
)
OPP = tuple(VEL.index(tuple(-e for e in v)) for v in VEL)
WEIGHT = (1.0 / 3.0,) + (1.0 / 18.0,) * 6 + (1.0 / 36.0,) * 12
X_UP, X_DN = (1, 7, 9, 11, 13), (2, 10, 8, 14, 12)
Y_UP, Y_DN = (3, 7, 10, 15, 17), (4, 9, 8, 18, 16)
Z_UP, Z_DN = (5, 11, 14, 15, 18), (6, 13, 12, 17, 16)
SX, SZ_, HALF = 4, 16, 128
DEPTH = 64
Z_S, Z_E, Z_ROWS = 40, 56, 64
Y_S, Y_E, Y_D, Y_ROWS = 16, 32, 40, 48
X_U, X_T, X_R, X_ROWS = 160, 416, 432, 440


def roll(value, shift, axis):
    size = value.shape[axis]
    shift = shift % size
    return value if shift == 0 else pltpu.roll(value, shift, axis)


def lanes(shape):
    return lax.broadcasted_iota(jnp.int32, shape, len(shape) - 1)


def rows_of(shape):
    return lax.broadcasted_iota(jnp.int32, shape, 0)


def collide(f):
    s = {i: f[i] + f[i + 1] for i in range(1, 19, 2)}
    d = {i: f[i] - f[i + 1] for i in range(1, 19, 2)}
    s_ab, s_ac, s_bc = s[7] + s[9], s[11] + s[13], s[15] + s[17]
    rho = (f[0] + s[1]) + (s[3] + s[5]) + (s_ab + s_ac + s_bc)
    m_a = d[1] + (d[7] + d[9]) + (d[11] + d[13])
    m_b = d[3] + (d[7] - d[9]) + (d[15] + d[17])
    m_c = d[5] + (d[11] - d[13]) + (d[15] - d[17])
    inv = 1.0 / rho
    u_a, u_b, u_c = m_a * inv, m_b * inv, m_c * inv
    p_aa, p_bb, p_cc = m_a * u_a, m_b * u_b, m_c * u_c
    p_ab, p_ac, p_bc = m_a * u_b, m_a * u_c, m_b * u_c
    q = p_aa + p_bb + p_cc
    base = rho - 1.5 * q
    t = rho - 2.0 * q
    t_ab = 4.0 * f[0] - 2.0 * (s[1] + s[3]) + s_ab - (t + 0.5 * p_cc)
    t_ac = 4.0 * f[0] - 2.0 * (s[1] + s[5]) + s_ac - (t + 0.5 * p_bb)
    t_bc = 4.0 * f[0] - 2.0 * (s[3] + s[5]) + s_bc - (t + 0.5 * p_aa)
    mean = (2.0 / 7.0) * (t_ab + t_ac + t_bc)
    gain = (SHEAR_RATE - EVEN_RATE) / 12.0
    c_ab, c_ac, c_bc = gain * (t_ab - mean), gain * (t_ac - mean), gain * (t_bc - mean)
    keep, half_keep, half = 1.0 - SHEAR_RATE, 0.5 * (1.0 - SHEAR_RATE), 0.5 * SHEAR_RATE
    odd, pull = 0.5 * (1.0 - ODD_RATE), 3.0 * ODD_RATE
    post = [None] * 19
    post[0] = keep * f[0] + (SHEAR_RATE / 3.0) * base + 4.0 * (c_ab + c_ac + c_bc)

    def put(i, extra, equil, moment, weight):
        even = half_keep * s[i] + equil + extra
        anti = odd * d[i] + (pull * weight) * moment
        post[i] = even + anti
        post[i + 1] = even - anti

    axis = half / 9.0
    for i, p, c, m in ((1, p_aa, c_ab + c_ac, m_a), (3, p_bb, c_ab + c_bc, m_b), (5, p_cc, c_ac + c_bc, m_c)):
        put(i, -2.0 * c, axis * (base + 4.5 * p), m, 1.0 / 18.0)
    diag = half / 18.0
    for i, pp, pq, c, m, n in (
        (7, p_aa + p_bb, p_ab, c_ab, m_a, m_b),
        (11, p_aa + p_cc, p_ac, c_ac, m_a, m_c),
        (15, p_bb + p_cc, p_bc, c_bc, m_b, m_c),
    ):
        even = diag * (base + 4.5 * pp)
        cross = (9.0 * diag) * pq
        put(i, c, even + cross, m + n, 1.0 / 36.0)
        put(i + 2, c, even - cross, m - n, 1.0 / 36.0)
    return post, q * inv


def face_kernel(pops, temp, cond, load, cool, zbuf, own, misc, tempv, condv, buf, sems):
    low = lax.axis_index("gz") == 0
    face = jnp.where(low, SZ_ - 1, 0)
    fields = [
        pltpu.make_async_copy(temp, tempv, sems.at[0]),
        pltpu.make_async_copy(cond, condv, sems.at[1]),
        pltpu.make_async_copy(load, misc.at[0:4], sems.at[2]),
        pltpu.make_async_copy(cool, misc.at[4:8], sems.at[3]),
    ]
    rows = []
    for k, layer in enumerate((face, 0)):
        for h in range(2):
            rows.append(pltpu.make_async_copy(
                pops.at[:, :, layer, HALF * h : HALF * h + HALF],
                buf.at[k, :, 4 * h : 4 * h + 4, :],
                sems.at[4 + 2 * k + h],
            ))
    for copy in rows + fields:
        copy.start()
    for copy in fields:
        copy.wait()
    lane = lanes((DEPTH, HALF))
    edges = jnp.zeros((DEPTH, HALF), F32)
    for k, field in enumerate((tempv, condv)):
        for x in range(SX):
            at = k * 16 + x * 4
            edges = jnp.where((lane >= at) & (lane < at + 4), roll(field[x], at + 2, 1), edges)
    own[...] = edges
    lane16 = lanes((16, HALF))
    fold = edges[0:16]
    for g in range(1, 4):
        fold = jnp.where(lane16 >= 32 * g, roll(edges[16 * g : 16 * g + 16], 32 * g, 1), fold)
    zbuf[Z_S : Z_S + 16, :] = fold
    for copy in rows:
        copy.wait()
    out, _ = collide([buf[0, v] for v in range(19)])
    for n in range(5):
        leaving = jnp.where(low, out[Z_UP[n]], out[Z_DN[n]])
        for h in range(2):
            zbuf[20 * h + 4 * n : 20 * h + 4 * n + 4, :] = leaving[4 * h : 4 * h + 4, :]
    _, speed = collide([buf[1, v] for v in range(19)])
    warm = H_BASE + H_GAIN * speed
    misc[8:16, :] = warm
    lane1 = lanes((1, HALF))
    row = jnp.zeros((1, HALF), F32)
    for k in range(4):
        for x in range(SX):
            at = k * 16 + x * 4
            value = misc[4 * k + x : 4 * k + x + 1, :]
            row = jnp.where((lane1 >= at) & (lane1 < at + 2), roll(value, at + 1, 1), row)
    zbuf[Z_E : Z_E + 4, :] = misc[12:16, :]
    zbuf[Z_E + 4 : Z_E + 5, :] = row
    zbuf[Z_E + 5 : Z_E + 8, :] = jnp.zeros((3, HALF), F32)


def collide_kernel(pops, nozzle, wall, tempv, condv, post, yp, ym, xp, xm, nozzlev, wallv, buf, sems):
    copies = [pltpu.make_async_copy(pops.at[:, x], buf.at[:, x], sems.at[x]) for x in range(SX)]
    plates = [
        pltpu.make_async_copy(nozzle, nozzlev, sems.at[SX]),
        pltpu.make_async_copy(wall, wallv, sems.at[SX + 1]),
    ]
    for copy in copies + plates:
        copy.start()
    for k, field in enumerate((tempv, condv)):
        for buffer, near, far in ((xp, 3, 2), (xm, 0, 1)):
            at = X_U + 128 * k
            buffer[at : at + 64, :] = field[near]
            buffer[at + 64 : at + 128, :] = field[far]
    y_up = [jnp.zeros((8, HALF), F32) for _ in range(2)]
    y_dn = [jnp.zeros((8, HALF), F32) for _ in range(2)]
    lane8 = lanes((8, HALF))
    for x in range(SX):
        copies[x].wait()
        for k in range(2):
            z = slice(8 * k, 8 * k + 8)
            for h in range(2):
                y = slice(HALF * h, HALF * h + HALF)
                out, _ = collide([buf[v, x, z, y] for v in range(19)])
                for v in range(19):
                    post[v, x, z, y] = out[v]
                for n in range(5):
                    at = 4 * n + x
                    if h == 1:
                        y_up[k] = jnp.where(lane8 == at, roll(out[Y_UP[n]], at - 127, 1), y_up[k])
                    else:
                        y_dn[k] = jnp.where(lane8 == at, roll(out[Y_DN[n]], at, 1), y_dn[k])
                    at = 32 * n + 16 * h + 8 * k
                    if x == 3:
                        xp[at : at + 8, :] = out[X_UP[n]]
                    if x == 0:
                        xm[at : at + 8, :] = out[X_DN[n]]
    for k in range(2):
        yp[8 * k : 8 * k + 8, :] = y_up[k]
        ym[8 * k : 8 * k + 8, :] = y_dn[k]
    for copy in plates:
        copy.wait()


def y_kernel(yp, ym, zbuf, zin, outp, outm):
    low = lax.axis_index("gz") == 0
    lane = lanes((1, HALF))
    sent = zin[Z_E + 4 : Z_E + 5, :]
    row = jnp.where((lane >= 32) & low, zbuf[Z_E + 4 : Z_E + 5, :], sent)
    for out, edge, first in ((outp, yp, 20 + 12), (outm, ym, 16)):
        out[0:16, :] = edge[...]
        out[Y_S : Y_S + 16, :] = zin[Z_S : Z_S + 16, :]
        out[Y_E : Y_E + 8, :] = jnp.broadcast_to(row, (8, HALF))
        out[Y_D : Y_D + 4, :] = zin[first : first + 4, :]
        out[Y_D + 4 : Y_D + 8, :] = jnp.zeros((4, HALF), F32)


def halo_slabs(low, zin, ypin, ymin):
    left = jnp.where(low, ypin[Y_S : Y_S + 16, :], zin[Z_S : Z_S + 16, :])
    right = jnp.where(low, zin[Z_S : Z_S + 16, :], ymin[Y_S : Y_S + 16, :])
    return left, right


def x_kernel(inp, inm, zin, ypin, ymin, misc, outp, outm):
    low = lax.axis_index("gz") == 0
    left, right = halo_slabs(low, zin, ypin, ymin)
    warm = jnp.where(low, misc[8:12, :], zin[Z_E : Z_E + 4, :])
    lane = lanes((16, HALF))
    for out, x, n, up, dn in ((outp, 3, 1, 7, 9), (outm, 0, 2, 10, 8)):
        k_up, k_dn = 4 * Y_UP.index(up) + x, 4 * Y_DN.index(dn) + x + 1
        slab = jnp.where((lane & 15) == 4 * x + 1, left, right)
        slab = jnp.where(lane == k_up, ypin[0:16, :], slab)
        out[X_T : X_T + 16, :] = jnp.where(lane == k_dn, roll(ymin[0:16, :], 1, 1), slab)
        for h in range(2):
            row = 20 * h + 4 * n + x
            out[X_R + h : X_R + h + 1, :] = zin[row : row + 1, :]
        out[X_R + 2 : X_R + 3, :] = misc[x : x + 1, :]
        out[X_R + 3 : X_R + 4, :] = misc[4 + x : 5 + x, :]
        out[X_R + 4 : X_R + 5, :] = warm[x : x + 1, :]
        out[X_R + 5 : X_R + 8, :] = jnp.zeros((3, HALF), F32)


def stream(v, x, low, post, zin, ypin, ymin, xpin, xmin, nozzle, wall):
    lane = lanes((SZ_, HALF))
    layer = rows_of((SZ_, HALF))
    a, b, c = VEL[v]
    s = x - a
    inside = 0 <= s < SX
    edge = xpin if s < 0 else xmin
    if inside:
        tiles = [post[v, s, :, HALF * h : HALF * h + HALF] for h in range(2)]
    else:
        n = (X_UP if s < 0 else X_DN).index(v)
        tiles = [edge[32 * n + 16 * h : 32 * n + 16 * h + 16, :] for h in range(2)]
    beside = None
    if b:
        slab = ypin if b > 0 else ymin
        k = 4 * (Y_UP if b > 0 else Y_DN).index(v)
        if inside:
            k, column = k + s, slab[0:16, :]
        else:
            k, column = k + (3 if s < 0 else 0) + (1 if b < 0 else 0), edge[X_T : X_T + 16, :]
        beside = roll(column, (0 if b > 0 else HALF - 1) - k, 1)
    if c:
        n = (Z_UP if c > 0 else Z_DN).index(v)
        at = 0 if c > 0 else SZ_ - 1
        for h in range(2):
            k = 20 * h + 4 * n + s
            row = zin[k : k + 1, :] if inside else edge[X_R + h : X_R + h + 1, :]
            tiles[h] = jnp.where(layer == at, row, roll(tiles[h], c, 0))
        if b:
            corner = roll(slab[Y_D + x : Y_D + x + 1, :], b, 1)
            beside = jnp.where(layer == at, corner, roll(beside, c, 0))
    if b > 0:
        t0, t1 = roll(tiles[0], 1, 1), roll(tiles[1], 1, 1)
        tiles = [jnp.where(lane == 0, beside, t0), jnp.where(lane == 0, t0, t1)]
    elif b < 0:
        t0, t1 = roll(tiles[0], -1, 1), roll(tiles[1], -1, 1)
        tiles = [jnp.where(lane == HALF - 1, t1, t0), jnp.where(lane == HALF - 1, beside, t1)]
    for h in range(2):
        y = slice(HALF * h, HALF * h + HALF)
        if c > 0:
            back = post[OPP[v], x, 0:1, y]
            tiles[h] = jnp.where((layer == 0) & low, back, tiles[h])
        elif c < 0:
            back = post[OPP[v], x, SZ_ - 1 : SZ_, y]
            through = post[v, x, SZ_ - 1 : SZ_, y]
            top = jnp.where(
                nozzle[x : x + 1, y] == 1,
                back + 6.0 * WEIGHT[v] * JET_SPEED,
                jnp.where(wall[x : x + 1, y] == 1, through, back),
            )
            tiles[h] = jnp.where((layer == SZ_ - 1) & jnp.logical_not(low), top, tiles[h])
    return tiles


INNER = tuple(v for v in range(19) if VEL[v][1] == 0)
SIDE = tuple(v for v in range(19) if VEL[v][1] != 0)


def put_inside(velocities, low, out, buf, sems, *state):
    copies = []
    for i, v in enumerate(velocities):
        a = VEL[v][0]
        first, last = max(a, 0), SX + min(a, 0)
        for x in range(first, last):
            for h, tile in enumerate(stream(v, x, low, *state)):
                buf[i, x, :, HALF * h : HALF * h + HALF] = tile
        copy = pltpu.make_async_copy(buf.at[i, first:last], out.at[v, first:last], sems.at[i])
        copy.start()
        copies.append(copy)
    for copy in copies:
        copy.wait()


def inner_kernel(post, zin, nozzle, wall, out, buf, sems):
    low = lax.axis_index("gz") == 0
    put_inside(INNER, low, out, buf, sems, post, zin, None, None, None, None, nozzle, wall)


def side_kernel(whole, post, zin, ypin, ymin, nozzle, wall, out, buf, sems):
    low = lax.axis_index("gz") == 0
    put_inside(SIDE, low, out, buf, sems, post, zin, ypin, ymin, None, None, nozzle, wall)


def final_kernel(
    whole, post, zin, ypin, ymin, xpin, xmin, nozzle, wall, temp, cond, own, misc, zbuf,
    pops_out, solid_out, buf, solid, sems,
):
    low = lax.axis_index("gz") == 0
    copies = []
    for i, v in enumerate(X_UP + X_DN):
        x = 0 if i < 5 else SX - 1
        for h, tile in enumerate(stream(v, x, low, post, zin, ypin, ymin, xpin, xmin, nozzle, wall)):
            buf[i, :, HALF * h : HALF * h + HALF] = tile
        copies.append(pltpu.make_async_copy(buf.at[i], pops_out.at[v, x], sems.at[i]))
        copies[-1].start()

    lane = lanes((DEPTH, HALF))
    depth = rows_of((DEPTH, HALF))
    floor, face = depth == 0, depth == DEPTH - 1

    def spread(folded, at):
        return jnp.concatenate([roll(folded, at - 32 * g, 1) for g in range(4)], axis=0)

    def vertical(c):
        down = jnp.where(face, 0.0, 0.5 * (c + roll(c, -1, 0)))
        return down, roll(down, 1, 0)

    def around(links):
        total = None
        for link, value in links:
            total = link * value if total is None else total + link * value
        return total

    U = {x: temp[x] for x in range(SX)}
    C = {x: cond[x] for x in range(SX)}
    for near, far, edge in ((-1, -2, xpin), (4, 5, xmin)):
        U[near], U[far] = edge[X_U : X_U + 64, :], edge[X_U + 64 : X_U + 128, :]
        C[near], C[far] = edge[X_U + 128 : X_U + 192, :], edge[X_U + 192 : X_U + 256, :]
    warm = jnp.where(low, misc[8:12, :], zin[Z_E : Z_E + 4, :])
    loads = {x: misc[x : x + 1, :] for x in range(SX)}
    cools = {x: misc[4 + x : 5 + x, :] for x in range(SX)}
    warms = {x: warm[x : x + 1, :] for x in range(SX)}
    for x, edge in ((-1, xpin), (4, xmin)):
        loads[x], cools[x], warms[x] = (edge[X_R + 2 + k : X_R + 3 + k, :] for k in range(3))

    left, right = halo_slabs(low, zin, ypin, ymin)
    own_edges = own[...]
    near_first = {}
    side = {}
    row_left = jnp.where(low, ypin[Y_E : Y_E + 1, :], zin[Z_E + 4 : Z_E + 5, :])
    row_right = jnp.where(low, zin[Z_E + 4 : Z_E + 5, :], ymin[Y_E : Y_E + 1, :])
    heat_left = jnp.where(low, roll(row_left, -48, 1), roll(row_left, -32, 1))
    heat_right = jnp.where(low, roll(zbuf[Z_E + 4 : Z_E + 5, :], -49, 1), roll(row_right, -33, 1))
    before, after = xpin[X_T : X_T + 16, :], xmin[X_T : X_T + 16, :]
    for name, folded, j1, j2, jo, row, h_row, jr in (
        ("left", left, 1, 0, 2, row_left, heat_left, 0),
        ("right", right, 2, 3, 1, row_right, heat_right, 1),
    ):
        u1, u2 = spread(folded, -j1), spread(folded, -j2)
        c1, c2 = spread(folded, -16 - j1), spread(folded, -16 - j2)
        u1 = jnp.where(lane == 124, spread(before, 124 - 12 - j1), jnp.where(lane == 16, spread(after, 16 - j1), u1))
        c1 = jnp.where(lane == 124, spread(before, 124 - 28 - j1), jnp.where(lane == 16, spread(after, -j1), c1))
        side[name] = (u1, c1)
        uo, co = roll(own_edges, -jo, 1), roll(own_edges, -16 - jo, 1)
        g_far, g_own = 0.5 * (c1 + c2), 0.5 * (c1 + co)
        g_up = 0.5 * (c1 + roll(c1, -4, 1))
        g_dn = roll(g_up, 4, 1)
        v_dn, v_up = vertical(c1)
        e_load, e_cool = roll(row, -jr, 1), roll(row, -16 - jr, 1)
        num = u1 + jnp.where(floor, e_load, 0.0) + jnp.where(face, h_row * e_cool, 0.0)
        den = 1.0 + jnp.where(face, h_row, 0.0) + (g_far + g_own) + (g_up + g_dn) + (v_dn + v_up)
        num = num + around(((g_far, u2), (g_own, uo), (g_up, roll(u1, -4, 1)), (g_dn, roll(u1, 4, 1)),
                            (v_dn, roll(u1, -1, 0)), (v_up, roll(u1, 1, 0))))
        near_first[name] = num / den

    def beside_of(value, left_col, right_col):
        return (
            jnp.where(lane == 0, left_col, roll(value, 1, 1)),
            jnp.where(lane == HALF - 1, right_col, roll(value, -1, 1)),
        )

    def columns(pair, x):
        at = (4 * x) % HALF
        return roll(pair[0], -at, 1), roll(pair[1], HALF - 1 - at, 1)

    pair_u = (side["left"][0], side["right"][0])
    pair_c = (side["left"][1], side["right"][1])
    pair_f = (near_first["left"], near_first["right"])
    g_x = {x: 0.5 * (C[x] + C[x + 1]) for x in range(-2, 5)}
    first, kept = {}, {}
    for x in range(-1, 5):
        c_l, c_r = beside_of(C[x], *columns(pair_c, x))
        u_l, u_r = beside_of(U[x], *columns(pair_u, x))
        g_l, g_r = 0.5 * (C[x] + c_l), 0.5 * (C[x] + c_r)
        v_dn, v_up = vertical(C[x])
        base = U[x] + jnp.where(floor, loads[x], 0.0) + jnp.where(face, warms[x] * cools[x], 0.0)
        den = 1.0 + jnp.where(face, warms[x], 0.0) + (g_x[x - 1] + g_x[x]) + (g_l + g_r) + (v_dn + v_up)
        inv = 1.0 / den
        num = base + around(((g_x[x - 1], U[x - 1]), (g_x[x], U[x + 1]), (g_l, u_l), (g_r, u_r),
                             (v_dn, roll(U[x], -1, 0)), (v_up, roll(U[x], 1, 0))))
        first[x] = num * inv
        kept[x] = (base, inv, g_l, g_r, v_dn, v_up)
    for x in range(SX):
        base, inv, g_l, g_r, v_dn, v_up = kept[x]
        f_l, f_r = beside_of(first[x], *columns(pair_f, x))
        num = base + around(((g_x[x - 1], first[x - 1]), (g_x[x], first[x + 1]), (g_l, f_l), (g_r, f_r),
                             (v_dn, roll(first[x], -1, 0)), (v_up, roll(first[x], 1, 0))))
        solid[x] = num * inv
        copies.append(pltpu.make_async_copy(solid.at[x], solid_out.at[x], sems.at[10 + x]))
        copies[-1].start()
    for copy in copies:
        copy.wait()


def shape(*dims):
    return jax.ShapeDtypeStruct(dims, F32)


def near(*dims):
    return pltpu.VMEM(dims, F32)


def hold(*arrays):
    return [pltpu.with_memory_space_constraint(a, pltpu.VMEM) for a in arrays]


VM = pl.BlockSpec(memory_space=pltpu.VMEM)
ANY = pl.BlockSpec(memory_space=pl.ANY)


def ring(axis, step):
    n = lax.axis_size(axis)
    return [(i, (i + step) % n) for i in range(n)]


def call(kernel, name, inputs, outputs, scratch=(), aliases=None):
    spaces = [ANY if kind == "far" else VM for kind, _ in inputs]
    arrays = [hold(a)[0] if kind == "near" else a for kind, a in inputs]
    return pl.pallas_call(
        kernel,
        name=name,
        in_specs=spaces,
        out_specs=[ANY if isinstance(o, jax.ShapeDtypeStruct) else VM for o in outputs],
        out_shape=list(outputs),
        scratch_shapes=list(scratch),
        input_output_aliases=aliases or {},
    )(*arrays)


def far(*arrays):
    return [("far", a) for a in arrays]


def kept(*arrays):
    return [("near", a) for a in arrays]


def body(populations, nozzle_mask, wall_type, solid_temp, diffusion, heat_load, coolant_temp):
    dma = pltpu.SemaphoreType.DMA
    zbuf, own, misc, temp, cond = call(
        face_kernel, "face",
        far(populations, solid_temp, diffusion, heat_load, coolant_temp),
        [near(Z_ROWS, HALF), near(DEPTH, HALF), near(16, HALF), near(SX, DEPTH, HALF), near(SX, DEPTH, HALF)],
        [pltpu.VMEM((2, 19, 8, HALF), F32), dma((8,))],
    )
    zin = lax.ppermute(zbuf, "gz", ring("gz", 1))
    post, yp, ym, xp, xm, nozzle, wall = call(
        collide_kernel, "collide",
        far(populations, nozzle_mask, wall_type) + kept(temp, cond),
        [near(19, SX, SZ_, 2 * HALF), near(16, HALF), near(16, HALF), near(X_ROWS, HALF), near(X_ROWS, HALF),
         pltpu.VMEM((SX, 2 * HALF), jnp.int32), pltpu.VMEM((SX, 2 * HALF), jnp.int32)],
        [pltpu.VMEM((19, SX, SZ_, 2 * HALF), F32), dma((SX + 2,))],
    )
    ypo, ymo = call(y_kernel, "pack_y", kept(yp, ym, zbuf, zin), [near(Y_ROWS, HALF)] * 2)
    ypin = lax.ppermute(ypo, "gy", ring("gy", 1))
    ymin = lax.ppermute(ymo, "gy", ring("gy", -1))
    (pops,) = call(
        inner_kernel, "inner", kept(post, zin, nozzle, wall), [shape(19, SX, SZ_, 2 * HALF)],
        [pltpu.VMEM((len(INNER), SX, SZ_, 2 * HALF), F32), dma((len(INNER),))],
    )
    xpo, xmo = call(
        x_kernel, "pack_x", kept(xp, xm, zin, ypin, ymin, misc), [near(X_ROWS, HALF)] * 2, aliases={0: 0, 1: 1}
    )
    xpin = lax.ppermute(xpo, "gx", ring("gx", 1))
    xmin = lax.ppermute(xmo, "gx", ring("gx", -1))
    (pops,) = call(
        side_kernel, "side", far(pops) + kept(post, zin, ypin, ymin, nozzle, wall), [shape(19, SX, SZ_, 2 * HALF)],
        [pltpu.VMEM((len(SIDE), SX, SZ_, 2 * HALF), F32), dma((len(SIDE),))], {0: 0},
    )
    return tuple(call(
        final_kernel, "finish",
        far(pops) + kept(post, zin, ypin, ymin, xpin, xmin, nozzle, wall, temp, cond, own, misc, zbuf),
        [shape(19, SX, SZ_, 2 * HALF), shape(SX, DEPTH, HALF)],
        [pltpu.VMEM((10, SZ_, 2 * HALF), F32), pltpu.VMEM((SX, DEPTH, HALF), F32), dma((14,))], {0: 0},
    ))


def solution(mesh):
    placed = (
        P(None, "gx", "gz", "gy"),
        P("gx", "gy"),
        P("gx", "gy"),
        P("gx", None, ("gy", "gz")),
        P("gx", None, ("gy", "gz")),
        P("gx", ("gy", "gz")),
        P("gx", ("gy", "gz")),
    )
    return jax.shard_map(
        body,
        mesh=mesh,
        in_specs=placed,
        out_specs=(P(None, "gx", "gz", "gy"), P("gx", None, ("gy", "gz"))),
        check_vma=False,
    )
```

```python
import jax
import jax.numpy as jnp
from jax import lax
from jax.experimental import pallas as pl
from jax.experimental.pallas import tpu as pltpu
from jax.sharding import PartitionSpec as P

F32 = jnp.float32
JET_SPEED = 0.1
H_BASE = 0.5
H_GAIN = 40.0
SHEAR_RATE = 1.6
ODD_RATE = 1.2
EVEN_RATE = 1.4
VEL = (
    (0, 0, 0),
    (1, 0, 0), (-1, 0, 0), (0, 1, 0), (0, -1, 0), (0, 0, 1), (0, 0, -1),
    (1, 1, 0), (-1, -1, 0), (1, -1, 0), (-1, 1, 0),
    (1, 0, 1), (-1, 0, -1), (1, 0, -1), (-1, 0, 1),
    (0, 1, 1), (0, -1, -1), (0, 1, -1), (0, -1, 1),
)
OPP = tuple(VEL.index(tuple(-e for e in v)) for v in VEL)
WEIGHT = (1.0 / 3.0,) + (1.0 / 18.0,) * 6 + (1.0 / 36.0,) * 12
X_UP, X_DN = (1, 7, 9, 11, 13), (2, 10, 8, 14, 12)
Y_UP, Y_DN = (3, 7, 10, 15, 17), (4, 9, 8, 18, 16)
Z_UP, Z_DN = (5, 11, 14, 15, 18), (6, 13, 12, 17, 16)
SX, SZ_, HALF = 4, 16, 128
DEPTH = 64
Z_S, Z_E, Z_ROWS = 40, 56, 64
Y_S, Y_E, Y_D, Y_ROWS = 16, 32, 40, 48
X_U, X_T, X_R, X_ROWS = 160, 416, 432, 440


def roll(value, shift, axis):
    size = value.shape[axis]
    shift = shift % size
    return value if shift == 0 else pltpu.roll(value, shift, axis)


def lanes(shape):
    return lax.broadcasted_iota(jnp.int32, shape, len(shape) - 1)


def rows_of(shape):
    return lax.broadcasted_iota(jnp.int32, shape, 0)


def collide(f):
    s = {i: f[i] + f[i + 1] for i in range(1, 19, 2)}
    d = {i: f[i] - f[i + 1] for i in range(1, 19, 2)}
    s_ab, s_ac, s_bc = s[7] + s[9], s[11] + s[13], s[15] + s[17]
    rho = (f[0] + s[1]) + (s[3] + s[5]) + (s_ab + s_ac + s_bc)
    m_a = d[1] + (d[7] + d[9]) + (d[11] + d[13])
    m_b = d[3] + (d[7] - d[9]) + (d[15] + d[17])
    m_c = d[5] + (d[11] - d[13]) + (d[15] - d[17])
    inv = 1.0 / rho
    u_a, u_b, u_c = m_a * inv, m_b * inv, m_c * inv
    p_aa, p_bb, p_cc = m_a * u_a, m_b * u_b, m_c * u_c
    p_ab, p_ac, p_bc = m_a * u_b, m_a * u_c, m_b * u_c
    q = p_aa + p_bb + p_cc
    base = rho - 1.5 * q
    t = rho - 2.0 * q
    t_ab = 4.0 * f[0] - 2.0 * (s[1] + s[3]) + s_ab - (t + 0.5 * p_cc)
    t_ac = 4.0 * f[0] - 2.0 * (s[1] + s[5]) + s_ac - (t + 0.5 * p_bb)
    t_bc = 4.0 * f[0] - 2.0 * (s[3] + s[5]) + s_bc - (t + 0.5 * p_aa)
    mean = (2.0 / 7.0) * (t_ab + t_ac + t_bc)
    gain = (SHEAR_RATE - EVEN_RATE) / 12.0
    c_ab, c_ac, c_bc = gain * (t_ab - mean), gain * (t_ac - mean), gain * (t_bc - mean)
    keep, half_keep, half = 1.0 - SHEAR_RATE, 0.5 * (1.0 - SHEAR_RATE), 0.5 * SHEAR_RATE
    odd, pull = 0.5 * (1.0 - ODD_RATE), 3.0 * ODD_RATE
    post = [None] * 19
    post[0] = keep * f[0] + (SHEAR_RATE / 3.0) * base + 4.0 * (c_ab + c_ac + c_bc)

    def put(i, extra, equil, moment, weight):
        even = half_keep * s[i] + equil + extra
        anti = odd * d[i] + (pull * weight) * moment
        post[i] = even + anti
        post[i + 1] = even - anti

    axis = half / 9.0
    for i, p, c, m in ((1, p_aa, c_ab + c_ac, m_a), (3, p_bb, c_ab + c_bc, m_b), (5, p_cc, c_ac + c_bc, m_c)):
        put(i, -2.0 * c, axis * (base + 4.5 * p), m, 1.0 / 18.0)
    diag = half / 18.0
    for i, pp, pq, c, m, n in (
        (7, p_aa + p_bb, p_ab, c_ab, m_a, m_b),
        (11, p_aa + p_cc, p_ac, c_ac, m_a, m_c),
        (15, p_bb + p_cc, p_bc, c_bc, m_b, m_c),
    ):
        even = diag * (base + 4.5 * pp)
        cross = (9.0 * diag) * pq
        put(i, c, even + cross, m + n, 1.0 / 36.0)
        put(i + 2, c, even - cross, m - n, 1.0 / 36.0)
    return post, q * inv


def even(axis):
    return (lax.axis_index(axis) & 1) == 0


def face_kernel(pops, temp, cond, load, cool, zbuf, own, misc, tempv, condv, buf, sems):
    low = lax.axis_index("gz") == 0
    face = jnp.where(low, SZ_ - 1, 0)
    fields = [
        pltpu.make_async_copy(temp, tempv, sems.at[0]),
        pltpu.make_async_copy(cond, condv, sems.at[1]),
        pltpu.make_async_copy(load, misc.at[0:4], sems.at[2]),
        pltpu.make_async_copy(cool, misc.at[4:8], sems.at[3]),
    ]
    rows = [
        [
            pltpu.make_async_copy(
                pops.at[:, :, layer, HALF * h : HALF * h + HALF],
                buf.at[k, :, 4 * h : 4 * h + 4, :],
                sems.at[4 + 2 * k + h],
            )
            for h in range(2)
        ]
        for k, layer in enumerate((face, 0))
    ]
    for copy in rows[0] + fields:
        copy.start()

    @pl.when(low)
    def _():
        for copy in rows[1]:
            copy.start()

    for copy in fields:
        copy.wait()
    lane = lanes((DEPTH, HALF))
    edges = jnp.zeros((DEPTH, HALF), F32)
    for k, field in enumerate((tempv, condv)):
        for x in range(SX):
            at = k * 16 + x * 4
            edges = jnp.where((lane >= at) & (lane < at + 4), roll(field[x], at + 2, 1), edges)
    own[...] = edges
    lane16 = lanes((16, HALF))
    fold = edges[0:16]
    for g in range(1, 4):
        fold = jnp.where(lane16 >= 32 * g, roll(edges[16 * g : 16 * g + 16], 32 * g, 1), fold)
    zbuf[Z_S : Z_S + 16, :] = fold
    for copy in rows[0]:
        copy.wait()
    out, _ = collide([buf[0, v] for v in range(19)])
    for n in range(5):
        leaving = jnp.where(low, out[Z_UP[n]], out[Z_DN[n]])
        for h in range(2):
            zbuf[20 * h + 4 * n : 20 * h + 4 * n + 4, :] = leaving[4 * h : 4 * h + 4, :]
    misc[8:16, :] = jnp.zeros((8, HALF), F32)

    @pl.when(low)
    def _():
        for copy in rows[1]:
            copy.wait()
        _, speed = collide([buf[1, v] for v in range(19)])
        misc[8:16, :] = H_BASE + H_GAIN * speed

    lane1 = lanes((1, HALF))
    row = jnp.zeros((1, HALF), F32)
    for k in range(4):
        for x in range(SX):
            at = k * 16 + x * 4
            value = misc[4 * k + x : 4 * k + x + 1, :]
            row = jnp.where((lane1 >= at) & (lane1 < at + 2), roll(value, at + 1, 1), row)
    zbuf[Z_E : Z_E + 4, :] = misc[12:16, :]
    zbuf[Z_E + 4 : Z_E + 5, :] = row
    zbuf[Z_E + 5 : Z_E + 8, :] = jnp.zeros((3, HALF), F32)


def collide_kernel(pops, nozzle, wall, tempv, condv, post, yp, ym, xa, xb, nozzlev, wallv, buf, face, sems):
    copies = [pltpu.make_async_copy(pops.at[:, x], buf.at[:, x], sems.at[x]) for x in range(SX)]
    plates = [
        pltpu.make_async_copy(nozzle, nozzlev, sems.at[SX]),
        pltpu.make_async_copy(wall, wallv, sems.at[SX + 1]),
    ]
    for copy in copies + plates:
        copy.start()
    paired = even("gx")
    for k, field in enumerate((tempv, condv)):
        for j in range(2):
            at = X_U + 128 * k + 64 * j
            up, dn = field[3 - j], field[j]
            xa[at : at + 64, :] = jnp.where(paired, up, dn)
            xb[at : at + 64, :] = jnp.where(paired, dn, up)
    y_up = [jnp.zeros((8, HALF), F32) for _ in range(2)]
    y_dn = [jnp.zeros((8, HALF), F32) for _ in range(2)]
    lane8 = lanes((8, HALF))
    for x in range(SX):
        copies[x].wait()
        for k in range(2):
            z = slice(8 * k, 8 * k + 8)
            for h in range(2):
                y = slice(HALF * h, HALF * h + HALF)
                out, _ = collide([buf[v, x, z, y] for v in range(19)])
                for v in range(19):
                    post[v, x, z, y] = out[v]
                for n in range(5):
                    at = 4 * n + x
                    if h == 1:
                        y_up[k] = jnp.where(lane8 == at, roll(out[Y_UP[n]], at - 127, 1), y_up[k])
                    else:
                        y_dn[k] = jnp.where(lane8 == at, roll(out[Y_DN[n]], at, 1), y_dn[k])
                    at = 32 * n + 16 * h + 8 * k
                    if x == 3:
                        up, dn = out[X_UP[n]], face[at : at + 8, :]
                        xa[at : at + 8, :] = jnp.where(paired, up, dn)
                        xb[at : at + 8, :] = jnp.where(paired, dn, up)
                    if x == 0:
                        face[at : at + 8, :] = out[X_DN[n]]
    for k in range(2):
        yp[8 * k : 8 * k + 8, :] = y_up[k]
        ym[8 * k : 8 * k + 8, :] = y_dn[k]
    for copy in plates:
        copy.wait()


def y_kernel(yp, ym, zbuf, zin, outa, outb):
    low = lax.axis_index("gz") == 0
    paired = even("gy")
    lane = lanes((1, HALF))
    sent = zin[Z_E + 4 : Z_E + 5, :]
    row = jnp.where((lane >= 32) & low, zbuf[Z_E + 4 : Z_E + 5, :], sent)
    up, dn = yp[...], ym[...]
    c_up, c_dn = zin[32:36, :], zin[16:20, :]
    for out, own_up in ((outa, paired), (outb, jnp.logical_not(paired))):
        out[0:16, :] = jnp.where(own_up, up, dn)
        out[Y_S : Y_S + 16, :] = zin[Z_S : Z_S + 16, :]
        out[Y_E : Y_E + 8, :] = jnp.broadcast_to(row, (8, HALF))
        out[Y_D : Y_D + 4, :] = jnp.where(own_up, c_up, c_dn)
        out[Y_D + 4 : Y_D + 8, :] = jnp.zeros((4, HALF), F32)


def halo_slabs(low, zin, ypin, ymin):
    left = jnp.where(low, ypin[Y_S : Y_S + 16, :], zin[Z_S : Z_S + 16, :])
    right = jnp.where(low, zin[Z_S : Z_S + 16, :], ymin[Y_S : Y_S + 16, :])
    return left, right


def x_kernel(ina, inb, zin, ya, yb, misc, pops, outa, outb, ypin, ymin):
    low = lax.axis_index("gz") == 0
    paired = even("gy")
    ypin[...] = jnp.where(paired, yb[...], ya[...])
    ymin[...] = jnp.where(paired, ya[...], yb[...])
    left, right = halo_slabs(low, zin, ypin, ymin)
    warm = jnp.where(low, misc[8:12, :], zin[Z_E : Z_E + 4, :])
    lane = lanes((16, HALF))
    tails = []
    for x, n, up, dn in ((3, 1, 7, 9), (0, 2, 10, 8)):
        k_up, k_dn = 4 * Y_UP.index(up) + x, 4 * Y_DN.index(dn) + x + 1
        slab = jnp.where((lane & 15) == 4 * x + 1, left, right)
        slab = jnp.where(lane == k_up, ypin[0:16, :], slab)
        slab = jnp.where(lane == k_dn, roll(ymin[0:16, :], 1, 1), slab)
        at = 4 * n + x
        tails.append((slab, zin[at : at + 1, :], zin[20 + at : 21 + at, :],
                      misc[x : x + 1, :], misc[4 + x : 5 + x, :], warm[x : x + 1, :]))
    paired = even("gx")
    for out, (first, second) in ((outa, (0, 1)), (outb, (1, 0))):
        parts = [jnp.where(paired, u, v) for u, v in zip(tails[first], tails[second])]
        out[X_T : X_T + 16, :] = parts[0]
        for k in range(5):
            out[X_R + k : X_R + k + 1, :] = parts[1 + k]
        out[X_R + 5 : X_R + 8, :] = jnp.zeros((3, HALF), F32)


def stream(v, x, low, post, zin, ypin, ymin, xpin, xmin, nozzle, wall):
    lane = lanes((SZ_, HALF))
    layer = rows_of((SZ_, HALF))
    a, b, c = VEL[v]
    s = x - a
    inside = 0 <= s < SX
    edge = xpin if s < 0 else xmin
    if inside:
        tiles = [post[v, s, :, HALF * h : HALF * h + HALF] for h in range(2)]
    else:
        n = (X_UP if s < 0 else X_DN).index(v)
        tiles = [edge[32 * n + 16 * h : 32 * n + 16 * h + 16, :] for h in range(2)]
    beside = None
    if b:
        slab = ypin if b > 0 else ymin
        k = 4 * (Y_UP if b > 0 else Y_DN).index(v)
        if inside:
            k, column = k + s, slab[0:16, :]
        else:
            k, column = k + (3 if s < 0 else 0) + (1 if b < 0 else 0), edge[X_T : X_T + 16, :]
        beside = roll(column, (0 if b > 0 else HALF - 1) - k, 1)
    if c:
        n = (Z_UP if c > 0 else Z_DN).index(v)
        at = 0 if c > 0 else SZ_ - 1
        for h in range(2):
            k = 20 * h + 4 * n + s
            row = zin[k : k + 1, :] if inside else edge[X_R + h : X_R + h + 1, :]
            tiles[h] = jnp.where(layer == at, row, roll(tiles[h], c, 0))
        if b:
            corner = roll(slab[Y_D + x : Y_D + x + 1, :], b, 1)
            beside = jnp.where(layer == at, corner, roll(beside, c, 0))
    if b > 0:
        t0, t1 = roll(tiles[0], 1, 1), roll(tiles[1], 1, 1)
        tiles = [jnp.where(lane == 0, beside, t0), jnp.where(lane == 0, t0, t1)]
    elif b < 0:
        t0, t1 = roll(tiles[0], -1, 1), roll(tiles[1], -1, 1)
        tiles = [jnp.where(lane == HALF - 1, t1, t0), jnp.where(lane == HALF - 1, beside, t1)]
    for h in range(2):
        y = slice(HALF * h, HALF * h + HALF)
        if c > 0:
            back = post[OPP[v], x, 0:1, y]
            tiles[h] = jnp.where((layer == 0) & low, back, tiles[h])
        elif c < 0:
            back = post[OPP[v], x, SZ_ - 1 : SZ_, y]
            through = post[v, x, SZ_ - 1 : SZ_, y]
            top = jnp.where(
                nozzle[x : x + 1, y] == 1,
                back + 6.0 * WEIGHT[v] * JET_SPEED,
                jnp.where(wall[x : x + 1, y] == 1, through, back),
            )
            tiles[h] = jnp.where((layer == SZ_ - 1) & jnp.logical_not(low), top, tiles[h])
    return tiles


INNER = tuple(v for v in range(19) if VEL[v][1] == 0)
SIDE = tuple(v for v in range(19) if VEL[v][1] != 0)


def put_inside(velocities, low, out, buf, sems, *state):
    copies = []
    for i, v in enumerate(velocities):
        a = VEL[v][0]
        first, last = max(a, 0), SX + min(a, 0)
        for x in range(first, last):
            for h, tile in enumerate(stream(v, x, low, *state)):
                buf[i, x, :, HALF * h : HALF * h + HALF] = tile
        copy = pltpu.make_async_copy(buf.at[i, first:last], out.at[v, first:last], sems.at[i])
        copy.start()
        copies.append(copy)
    for copy in copies:
        copy.wait()


def inner_kernel(post, zin, nozzle, wall, out, buf, sems):
    low = lax.axis_index("gz") == 0
    put_inside(INNER, low, out, buf, sems, post, zin, None, None, None, None, nozzle, wall)


def side_kernel(whole, post, zin, ypin, ymin, nozzle, wall, out, buf, sems):
    low = lax.axis_index("gz") == 0
    put_inside(SIDE, low, out, buf, sems, post, zin, ypin, ymin, None, None, nozzle, wall)


def spread(folded, at):
    return jnp.concatenate([roll(folded, at - 32 * g, 1) for g in range(4)], axis=0)


def vertical(c):
    down = jnp.where(rows_of((DEPTH, HALF)) == DEPTH - 1, 0.0, 0.5 * (c + roll(c, -1, 0)))
    return down, roll(down, 1, 0)


def around(*links):
    total = None
    for link, value in links:
        total = link * value if total is None else total + link * value
    return total


def beside_of(value, left_col, right_col):
    lane = lanes((DEPTH, HALF))
    return (
        jnp.where(lane == 0, left_col, roll(value, 1, 1)),
        jnp.where(lane == HALF - 1, right_col, roll(value, -1, 1)),
    )


def columns(pair, x):
    at = (4 * x) % HALF
    return roll(pair[0], -at, 1), roll(pair[1], HALF - 1 - at, 1)


def sources(u, load, cool, warm):
    depth = rows_of((DEPTH, HALF))
    floor, face = depth == 0, depth == DEPTH - 1
    base = u + jnp.where(floor, load, 0.0) + jnp.where(face, warm * cool, 0.0)
    return base, 1.0 + jnp.where(face, warm, 0.0)


def sink_kernel(temp, cond, own, misc, zbuf, zin, ypin, ymin, cell, edge):
    low = lax.axis_index("gz") == 0
    lane = lanes((DEPTH, HALF))
    left, right = halo_slabs(low, zin, ypin, ymin)
    own_edges = own[...]
    row_left = jnp.where(low, ypin[Y_E : Y_E + 1, :], zin[Z_E + 4 : Z_E + 5, :])
    row_right = jnp.where(low, zin[Z_E + 4 : Z_E + 5, :], ymin[Y_E : Y_E + 1, :])
    heat_left = jnp.where(low, roll(row_left, -48, 1), roll(row_left, -32, 1))
    heat_right = jnp.where(low, roll(zbuf[Z_E + 4 : Z_E + 5, :], -49, 1), roll(row_right, -33, 1))
    pair_u, pair_c, pair_f = [], [], []
    for side, (folded, j1, j2, jo, row, h_row, jr) in enumerate((
        (left, 1, 0, 2, row_left, heat_left, 0),
        (right, 2, 3, 1, row_right, heat_right, 1),
    )):
        u1, u2 = spread(folded, -j1), spread(folded, -j2)
        c1, c2 = spread(folded, -16 - j1), spread(folded, -16 - j2)
        uo, co = roll(own_edges, -jo, 1), roll(own_edges, -16 - jo, 1)
        g_far, g_own = 0.5 * (c1 + c2), 0.5 * (c1 + co)
        g_up = jnp.where(lane < 12, 0.5 * (c1 + roll(c1, -4, 1)), 0.0)
        g_dn = jnp.where(lane >= 4, roll(g_up, 4, 1), 0.0)
        v_dn, v_up = vertical(c1)
        base, rest = sources(u1, roll(row, -jr, 1), roll(row, -16 - jr, 1), h_row)
        den = rest + (g_far + g_own) + (g_up + g_dn) + (v_dn + v_up)
        num = base + around((g_far, u2), (g_own, uo), (g_up, roll(u1, -4, 1)), (g_dn, roll(u1, 4, 1)),
                            (v_dn, roll(u1, -1, 0)), (v_up, roll(u1, 1, 0)))
        edge[side, 0], edge[side, 1], edge[side, 2], edge[side, 3] = u1, c1, num, den
        pair_u.append(u1)
        pair_c.append(c1)
        pair_f.append(num / den)
    warm = jnp.where(low, misc[8:12, :], zin[Z_E : Z_E + 4, :])
    g_x = {x: 0.5 * (cond[x] + cond[x + 1]) for x in range(SX - 1)}
    first, inverse = {}, {}
    for x in range(SX):
        u, c = temp[x], cond[x]
        c_l, c_r = beside_of(c, *columns(pair_c, x))
        u_l, u_r = beside_of(u, *columns(pair_u, x))
        g_l, g_r = 0.5 * (c + c_l), 0.5 * (c + c_r)
        v_dn, v_up = vertical(c)
        base, den = sources(u, misc[x : x + 1, :], misc[4 + x : 5 + x, :], warm[x : x + 1, :])
        den = den + (g_l + g_r) + (v_dn + v_up)
        num = base + around((g_l, u_l), (g_r, u_r), (v_dn, roll(u, -1, 0)), (v_up, roll(u, 1, 0)))
        if x > 0:
            den, num = den + g_x[x - 1], num + g_x[x - 1] * temp[x - 1]
        if x < SX - 1:
            den, num = den + g_x[x], num + g_x[x] * temp[x + 1]
        for k, value in enumerate((num, den, base, g_l, g_r, v_dn)):
            cell[k, x] = value
        if 0 < x < SX - 1:
            inverse[x] = 1.0 / den
            first[x] = num * inverse[x]
    for x, other in ((1, 2), (2, 1)):
        f = first[x]
        f_l, f_r = beside_of(f, *columns(pair_f, x))
        v_dn = cell[5, x]
        num = cell[2, x] + g_x[1] * first[other] + around(
            (cell[3, x], f_l), (cell[4, x], f_r), (v_dn, roll(f, -1, 0)), (roll(v_dn, 1, 0), roll(f, 1, 0)))
        cell[0, x], cell[1, x], cell[2, x] = f, inverse[x], num


def final_kernel(
    whole, post, zin, ypin, ymin, xb, xa, nozzle, wall, temp, cond, cell, edges,
    pops_out, solid_out, xpin, xmin, buf, solid, sems,
):
    low = lax.axis_index("gz") == 0
    paired = even("gx")
    xpin[...] = jnp.where(paired, xb[...], xa[...])
    xmin[...] = jnp.where(paired, xa[...], xb[...])
    copies = []
    for i, v in enumerate(X_UP + X_DN):
        x = 0 if i < 5 else SX - 1
        for h, tile in enumerate(stream(v, x, low, post, zin, ypin, ymin, xpin, xmin, nozzle, wall)):
            buf[i, :, HALF * h : HALF * h + HALF] = tile
        copies.append(pltpu.make_async_copy(buf.at[i], pops_out.at[v, x], sems.at[i]))
        copies[-1].start()

    lane = lanes((DEPTH, HALF))
    before, after = xpin[X_T : X_T + 16, :], xmin[X_T : X_T + 16, :]
    pair_u, pair_c, pair_f = [], [], []
    for side, j in ((0, 1), (1, 2)):
        u1, c1 = edges[side, 0], edges[side, 1]
        u1 = jnp.where(lane == 124, spread(before, 112 - j), jnp.where(lane == 16, spread(after, 16 - j), u1))
        c1 = jnp.where(lane == 124, spread(before, 96 - j), jnp.where(lane == 16, spread(after, -j), c1))
        g_up = 0.5 * (c1 + roll(c1, -4, 1))
        g_dn = jnp.where(lane == 0, roll(g_up, 4, 1), 0.0)
        g_up = jnp.where(lane == 12, g_up, 0.0)
        num = edges[side, 2] + around((g_up, roll(u1, -4, 1)), (g_dn, roll(u1, 4, 1)))
        pair_u.append(u1)
        pair_c.append(c1)
        pair_f.append(num / (edges[side, 3] + g_up + g_dn))
    first, inverse, g_x = {1: cell[0, 1], 2: cell[0, 2]}, {1: cell[1, 1], 2: cell[1, 2]}, {}
    for side, x, n, inner in ((xpin, -1, 0, 1), (xmin, 4, 3, 2)):
        u, u_far = side[X_U : X_U + 64, :], side[X_U + 64 : X_U + 128, :]
        c, c_far = side[X_U + 128 : X_U + 192, :], side[X_U + 192 : X_U + 256, :]
        link, g_far = 0.5 * (c + cond[n]), 0.5 * (c + c_far)
        c_l, c_r = beside_of(c, *columns(pair_c, x))
        u_l, u_r = beside_of(u, *columns(pair_u, x))
        g_l, g_r = 0.5 * (c + c_l), 0.5 * (c + c_r)
        v_dn, v_up = vertical(c)
        base, den = sources(u, *(side[X_R + 2 + k : X_R + 3 + k, :] for k in range(3)))
        den = den + (link + g_far) + (g_l + g_r) + (v_dn + v_up)
        num = base + around((g_far, u_far), (link, temp[n]), (g_l, u_l), (g_r, u_r),
                            (v_dn, roll(u, -1, 0)), (v_up, roll(u, 1, 0)))
        outer = num / den
        inverse[n] = 1.0 / (cell[1, n] + link)
        first[n] = (cell[0, n] + link * u) * inverse[n]
        f = first[n]
        f_l, f_r = beside_of(f, *columns(pair_f, n))
        v_dn = cell[5, n]
        g_x[inner] = 0.5 * (cond[n] + cond[inner])
        num = cell[2, n] + link * outer + g_x[inner] * first[inner] + around(
            (cell[3, n], f_l), (cell[4, n], f_r), (v_dn, roll(f, -1, 0)), (roll(v_dn, 1, 0), roll(f, 1, 0)))
        solid[n] = num * inverse[n]
        solid[inner] = (cell[2, inner] + g_x[inner] * f) * inverse[inner]
        for k in (n, inner):
            copies.append(pltpu.make_async_copy(solid.at[k], solid_out.at[k], sems.at[10 + k]))
            copies[-1].start()
    for copy in copies:
        copy.wait()


def shape(*dims):
    return pltpu.HBM(dims, F32)


def near(*dims):
    return pltpu.VMEM(dims, F32)


def hold(array, kind):
    return pltpu.with_memory_space_constraint(array, pltpu.VMEM if kind == "near" else pltpu.HBM)


VM = pl.BlockSpec(memory_space=pltpu.VMEM)
ANY = pl.BlockSpec(memory_space=pl.ANY)


def ring(axis, step):
    n = lax.axis_size(axis)
    return [(i, (i + step) % n) for i in range(n)]


def pairs(axis, odd):
    n = lax.axis_size(axis)
    return [(i, (i + 1) % n if i % 2 == odd else (i - 1) % n) for i in range(n)]


def call(kernel, name, inputs, outputs, scratch=(), aliases=None):
    spaces = [ANY if kind == "far" else VM for kind, _ in inputs]
    arrays = [hold(a, kind) for kind, a in inputs]
    return pl.pallas_call(
        kernel,
        name=name,
        in_specs=spaces,
        out_specs=[ANY if o.memory_space == pltpu.HBM else VM for o in outputs],
        out_shape=list(outputs),
        scratch_shapes=list(scratch),
        input_output_aliases=aliases or {},
        compiler_params=pltpu.CompilerParams(vmem_limit_bytes=16 * 1024 * 1024),
    )(*arrays)


def far(*arrays):
    return [("far", a) for a in arrays]


def kept(*arrays):
    return [("near", a) for a in arrays]


def body(populations, nozzle_mask, wall_type, solid_temp, diffusion, heat_load, coolant_temp):
    dma = pltpu.SemaphoreType.DMA
    zbuf, own, misc, temp, cond = call(
        face_kernel, "face",
        far(populations, solid_temp, diffusion, heat_load, coolant_temp),
        [near(Z_ROWS, HALF), near(DEPTH, HALF), near(16, HALF), near(SX, DEPTH, HALF), near(SX, DEPTH, HALF)],
        [pltpu.VMEM((2, 19, 8, HALF), F32), dma((8,))],
    )
    zin = lax.ppermute(zbuf, "gz", ring("gz", 1))
    post, yp, ym, xa, xb, nozzle, wall = call(
        collide_kernel, "collide",
        far(populations, nozzle_mask, wall_type) + kept(temp, cond),
        [near(19, SX, SZ_, 2 * HALF), near(16, HALF), near(16, HALF), near(X_ROWS, HALF), near(X_ROWS, HALF),
         pltpu.VMEM((SX, 2 * HALF), jnp.int32), pltpu.VMEM((SX, 2 * HALF), jnp.int32)],
        [pltpu.VMEM((19, SX, SZ_, 2 * HALF), F32), pltpu.VMEM((X_U, HALF), F32), dma((SX + 2,))],
    )
    yao, ybo = call(y_kernel, "pack_y", kept(yp, ym, zbuf, zin), [near(Y_ROWS, HALF)] * 2)
    ya = lax.ppermute(yao, "gy", pairs("gy", 0))
    yb = lax.ppermute(ybo, "gy", pairs("gy", 1))
    (pops,) = call(
        inner_kernel, "inner", kept(post, zin, nozzle, wall), [shape(19, SX, SZ_, 2 * HALF)],
        [pltpu.VMEM((len(INNER), SX, SZ_, 2 * HALF), F32), dma((len(INNER),))],
    )
    xao, xbo, ypin, ymin = call(
        x_kernel, "pack_x", kept(xa, xb, zin, ya, yb, misc) + far(pops),
        [near(X_ROWS, HALF)] * 2 + [near(Y_ROWS, HALF)] * 2, aliases={0: 0, 1: 1},
    )
    xa = lax.ppermute(xao, "gx", pairs("gx", 0))
    xb = lax.ppermute(xbo, "gx", pairs("gx", 1))
    cell, edge = call(
        sink_kernel, "sink", kept(temp, cond, own, misc, zbuf, zin, ypin, ymin),
        [near(6, SX, DEPTH, HALF), near(2, 4, DEPTH, HALF)],
    )
    (pops,) = call(
        side_kernel, "side", far(pops) + kept(post, zin, ypin, ymin, nozzle, wall), [shape(19, SX, SZ_, 2 * HALF)],
        [pltpu.VMEM((len(SIDE), SX, SZ_, 2 * HALF), F32), dma((len(SIDE),))], {0: 0},
    )
    return tuple(call(
        final_kernel, "finish",
        far(pops) + kept(post, zin, ypin, ymin, xb, xa, nozzle, wall, temp, cond, cell, edge),
        [shape(19, SX, SZ_, 2 * HALF), shape(SX, DEPTH, HALF)],
        [pltpu.VMEM((X_ROWS, HALF), F32), pltpu.VMEM((X_ROWS, HALF), F32),
         pltpu.VMEM((10, SZ_, 2 * HALF), F32), pltpu.VMEM((SX, DEPTH, HALF), F32), dma((14,))], {0: 0},
    ))


def solution(mesh):
    placed = (
        P(None, "gx", "gz", "gy"),
        P("gx", "gy"),
        P("gx", "gy"),
        P("gx", None, ("gy", "gz")),
        P("gx", None, ("gy", "gz")),
        P("gx", ("gy", "gz")),
        P("gx", ("gy", "gz")),
    )
    return jax.shard_map(
        body,
        mesh=mesh,
        in_specs=placed,
        out_specs=(P(None, "gx", "gz", "gy"), P("gx", None, ("gy", "gz"))),
        check_vma=False,
    )
```

```python
import jax
import jax.numpy as jnp
from jax import lax
from jax.experimental import pallas as pl
from jax.experimental.pallas import tpu as pltpu
from jax.sharding import PartitionSpec as P

F32 = jnp.float32
JET_SPEED = 0.1
H_BASE = 0.5
H_GAIN = 40.0
SHEAR_RATE = 1.6
ODD_RATE = 1.2
EVEN_RATE = 1.4
VEL = (
    (0, 0, 0),
    (1, 0, 0), (-1, 0, 0), (0, 1, 0), (0, -1, 0), (0, 0, 1), (0, 0, -1),
    (1, 1, 0), (-1, -1, 0), (1, -1, 0), (-1, 1, 0),
    (1, 0, 1), (-1, 0, -1), (1, 0, -1), (-1, 0, 1),
    (0, 1, 1), (0, -1, -1), (0, 1, -1), (0, -1, 1),
)
OPP = tuple(VEL.index(tuple(-e for e in v)) for v in VEL)
WEIGHT = (1.0 / 3.0,) + (1.0 / 18.0,) * 6 + (1.0 / 36.0,) * 12
X_UP, X_DN = (1, 7, 9, 11, 13), (2, 10, 8, 14, 12)
Y_UP, Y_DN = (3, 7, 10, 15, 17), (4, 9, 8, 18, 16)
Z_UP, Z_DN = (5, 11, 14, 15, 18), (6, 13, 12, 17, 16)
SX, SZ_, HALF = 4, 16, 128
DEPTH = 64
Z_S, Z_E, Z_ROWS = 40, 56, 64
Y_S, Y_E, Y_D, Y_ROWS = 16, 32, 40, 48
X_U, X_T, X_R, X_ROWS = 160, 416, 432, 440


def roll(value, shift, axis):
    size = value.shape[axis]
    shift = shift % size
    return value if shift == 0 else pltpu.roll(value, shift, axis)


def lanes(shape):
    return lax.broadcasted_iota(jnp.int32, shape, len(shape) - 1)


def rows_of(shape):
    return lax.broadcasted_iota(jnp.int32, shape, 0)


def collide(f):
    s = {i: f[i] + f[i + 1] for i in range(1, 19, 2)}
    d = {i: f[i] - f[i + 1] for i in range(1, 19, 2)}
    s_ab, s_ac, s_bc = s[7] + s[9], s[11] + s[13], s[15] + s[17]
    rho = (f[0] + s[1]) + (s[3] + s[5]) + (s_ab + s_ac + s_bc)
    m_a = d[1] + (d[7] + d[9]) + (d[11] + d[13])
    m_b = d[3] + (d[7] - d[9]) + (d[15] + d[17])
    m_c = d[5] + (d[11] - d[13]) + (d[15] - d[17])
    inv = 1.0 / rho
    u_a, u_b, u_c = m_a * inv, m_b * inv, m_c * inv
    p_aa, p_bb, p_cc = m_a * u_a, m_b * u_b, m_c * u_c
    p_ab, p_ac, p_bc = m_a * u_b, m_a * u_c, m_b * u_c
    q = p_aa + p_bb + p_cc
    base = rho - 1.5 * q
    t = rho - 2.0 * q
    t_ab = 4.0 * f[0] - 2.0 * (s[1] + s[3]) + s_ab - (t + 0.5 * p_cc)
    t_ac = 4.0 * f[0] - 2.0 * (s[1] + s[5]) + s_ac - (t + 0.5 * p_bb)
    t_bc = 4.0 * f[0] - 2.0 * (s[3] + s[5]) + s_bc - (t + 0.5 * p_aa)
    mean = (2.0 / 7.0) * (t_ab + t_ac + t_bc)
    gain = (SHEAR_RATE - EVEN_RATE) / 12.0
    c_ab, c_ac, c_bc = gain * (t_ab - mean), gain * (t_ac - mean), gain * (t_bc - mean)
    keep, half_keep, half = 1.0 - SHEAR_RATE, 0.5 * (1.0 - SHEAR_RATE), 0.5 * SHEAR_RATE
    odd, pull = 0.5 * (1.0 - ODD_RATE), 3.0 * ODD_RATE
    post = [None] * 19
    post[0] = keep * f[0] + (SHEAR_RATE / 3.0) * base + 4.0 * (c_ab + c_ac + c_bc)

    def put(i, extra, equil, moment, weight):
        even = half_keep * s[i] + equil + extra
        anti = odd * d[i] + (pull * weight) * moment
        post[i] = even + anti
        post[i + 1] = even - anti

    axis = half / 9.0
    for i, p, c, m in ((1, p_aa, c_ab + c_ac, m_a), (3, p_bb, c_ab + c_bc, m_b), (5, p_cc, c_ac + c_bc, m_c)):
        put(i, -2.0 * c, axis * (base + 4.5 * p), m, 1.0 / 18.0)
    diag = half / 18.0
    for i, pp, pq, c, m, n in (
        (7, p_aa + p_bb, p_ab, c_ab, m_a, m_b),
        (11, p_aa + p_cc, p_ac, c_ac, m_a, m_c),
        (15, p_bb + p_cc, p_bc, c_bc, m_b, m_c),
    ):
        even = diag * (base + 4.5 * pp)
        cross = (9.0 * diag) * pq
        put(i, c, even + cross, m + n, 1.0 / 36.0)
        put(i + 2, c, even - cross, m - n, 1.0 / 36.0)
    return post, q * inv


def even(axis):
    return (lax.axis_index(axis) & 1) == 0


def odd_first(y):
    return (y < 2) | (y % 2 == 0)


def checker():
    odd = odd_first(lax.axis_index("gy"))
    return (lax.axis_index("gx") & 1) == jnp.where(odd, 1, 0)


def face_kernel(pops, temp, cond, load, cool, zbuf, own, misc, tempv, condv, buf, sems):
    low = lax.axis_index("gz") == 0
    face = jnp.where(low, SZ_ - 1, 0)
    fields = [
        pltpu.make_async_copy(temp, tempv, sems.at[0]),
        pltpu.make_async_copy(cond, condv, sems.at[1]),
        pltpu.make_async_copy(load, misc.at[0:4], sems.at[2]),
        pltpu.make_async_copy(cool, misc.at[4:8], sems.at[3]),
    ]
    rows = [
        [
            pltpu.make_async_copy(
                pops.at[:, :, layer, HALF * h : HALF * h + HALF],
                buf.at[k, :, 4 * h : 4 * h + 4, :],
                sems.at[4 + 2 * k + h],
            )
            for h in range(2)
        ]
        for k, layer in enumerate((face, 0))
    ]
    for copy in rows[0] + fields:
        copy.start()

    @pl.when(low)
    def _():
        for copy in rows[1]:
            copy.start()

    for copy in fields:
        copy.wait()
    lane = lanes((DEPTH, HALF))
    edges = jnp.zeros((DEPTH, HALF), F32)
    for k, field in enumerate((tempv, condv)):
        for x in range(SX):
            at = k * 16 + x * 4
            edges = jnp.where((lane >= at) & (lane < at + 4), roll(field[x], at + 2, 1), edges)
    own[...] = edges
    lane16 = lanes((16, HALF))
    fold = edges[0:16]
    for g in range(1, 4):
        fold = jnp.where(lane16 >= 32 * g, roll(edges[16 * g : 16 * g + 16], 32 * g, 1), fold)
    zbuf[Z_S : Z_S + 16, :] = fold
    for copy in rows[0]:
        copy.wait()
    out, _ = collide([buf[0, v] for v in range(19)])
    for n in range(5):
        leaving = jnp.where(low, out[Z_UP[n]], out[Z_DN[n]])
        for h in range(2):
            zbuf[20 * h + 4 * n : 20 * h + 4 * n + 4, :] = leaving[4 * h : 4 * h + 4, :]
    misc[8:16, :] = jnp.zeros((8, HALF), F32)

    @pl.when(low)
    def _():
        for copy in rows[1]:
            copy.wait()
        _, speed = collide([buf[1, v] for v in range(19)])
        misc[8:16, :] = H_BASE + H_GAIN * speed

    lane1 = lanes((1, HALF))
    row = jnp.zeros((1, HALF), F32)
    for k in range(4):
        for x in range(SX):
            at = k * 16 + x * 4
            value = misc[4 * k + x : 4 * k + x + 1, :]
            row = jnp.where((lane1 >= at) & (lane1 < at + 2), roll(value, at + 1, 1), row)
    zbuf[Z_E : Z_E + 4, :] = misc[12:16, :]
    zbuf[Z_E + 4 : Z_E + 5, :] = row
    zbuf[Z_E + 5 : Z_E + 8, :] = jnp.zeros((3, HALF), F32)


def collide_kernel(pops, nozzle, wall, tempv, condv, post, yp, ym, xa, xb, nozzlev, wallv, buf, face, sems):
    copies = [pltpu.make_async_copy(pops.at[:, x], buf.at[:, x], sems.at[x]) for x in range(SX)]
    plates = [
        pltpu.make_async_copy(nozzle, nozzlev, sems.at[SX]),
        pltpu.make_async_copy(wall, wallv, sems.at[SX + 1]),
    ]
    for copy in copies + plates:
        copy.start()
    paired = checker()
    for k, field in enumerate((tempv, condv)):
        for j in range(2):
            at = X_U + 128 * k + 64 * j
            up, dn = field[3 - j], field[j]
            xa[at : at + 64, :] = jnp.where(paired, up, dn)
            xb[at : at + 64, :] = jnp.where(paired, dn, up)
    y_up = [jnp.zeros((8, HALF), F32) for _ in range(2)]
    y_dn = [jnp.zeros((8, HALF), F32) for _ in range(2)]
    lane8 = lanes((8, HALF))
    for x in range(SX):
        copies[x].wait()
        for k in range(2):
            z = slice(8 * k, 8 * k + 8)
            for h in range(2):
                y = slice(HALF * h, HALF * h + HALF)
                out, _ = collide([buf[v, x, z, y] for v in range(19)])
                for v in range(19):
                    post[v, x, z, y] = out[v]
                for n in range(5):
                    at = 4 * n + x
                    if h == 1:
                        y_up[k] = jnp.where(lane8 == at, roll(out[Y_UP[n]], at - 127, 1), y_up[k])
                    else:
                        y_dn[k] = jnp.where(lane8 == at, roll(out[Y_DN[n]], at, 1), y_dn[k])
                    at = 32 * n + 16 * h + 8 * k
                    if x == 3:
                        up, dn = out[X_UP[n]], face[at : at + 8, :]
                        xa[at : at + 8, :] = jnp.where(paired, up, dn)
                        xb[at : at + 8, :] = jnp.where(paired, dn, up)
                    if x == 0:
                        face[at : at + 8, :] = out[X_DN[n]]
    for k in range(2):
        yp[8 * k : 8 * k + 8, :] = y_up[k]
        ym[8 * k : 8 * k + 8, :] = y_dn[k]
    for copy in plates:
        copy.wait()


def y_kernel(yp, ym, zbuf, zin, outa, outb):
    low = lax.axis_index("gz") == 0
    paired = even("gy")
    lane = lanes((1, HALF))
    sent = zin[Z_E + 4 : Z_E + 5, :]
    row = jnp.where((lane >= 32) & low, zbuf[Z_E + 4 : Z_E + 5, :], sent)
    up, dn = yp[...], ym[...]
    c_up, c_dn = zin[32:36, :], zin[16:20, :]
    for out, own_up in ((outa, paired), (outb, jnp.logical_not(paired))):
        out[0:16, :] = jnp.where(own_up, up, dn)
        out[Y_S : Y_S + 16, :] = zin[Z_S : Z_S + 16, :]
        out[Y_E : Y_E + 8, :] = jnp.broadcast_to(row, (8, HALF))
        out[Y_D : Y_D + 4, :] = jnp.where(own_up, c_up, c_dn)
        out[Y_D + 4 : Y_D + 8, :] = jnp.zeros((4, HALF), F32)


def halo_slabs(low, zin, ypin, ymin):
    left = jnp.where(low, ypin[Y_S : Y_S + 16, :], zin[Z_S : Z_S + 16, :])
    right = jnp.where(low, zin[Z_S : Z_S + 16, :], ymin[Y_S : Y_S + 16, :])
    return left, right


def x_kernel(ina, inb, zin, ya, yb, misc, pops, outa, outb, ypin, ymin):
    low = lax.axis_index("gz") == 0
    paired = even("gy")
    ypin[...] = jnp.where(paired, yb[...], ya[...])
    ymin[...] = jnp.where(paired, ya[...], yb[...])
    left, right = halo_slabs(low, zin, ypin, ymin)
    warm = jnp.where(low, misc[8:12, :], zin[Z_E : Z_E + 4, :])
    lane = lanes((16, HALF))
    tails = []
    for x, n, up, dn in ((3, 1, 7, 9), (0, 2, 10, 8)):
        k_up, k_dn = 4 * Y_UP.index(up) + x, 4 * Y_DN.index(dn) + x + 1
        slab = jnp.where((lane & 15) == 4 * x + 1, left, right)
        slab = jnp.where(lane == k_up, ypin[0:16, :], slab)
        slab = jnp.where(lane == k_dn, roll(ymin[0:16, :], 1, 1), slab)
        at = 4 * n + x
        tails.append((slab, zin[at : at + 1, :], zin[20 + at : 21 + at, :],
                      misc[x : x + 1, :], misc[4 + x : 5 + x, :], warm[x : x + 1, :]))
    paired = checker()
    for out, (first, second) in ((outa, (0, 1)), (outb, (1, 0))):
        parts = [jnp.where(paired, u, v) for u, v in zip(tails[first], tails[second])]
        out[X_T : X_T + 16, :] = parts[0]
        for k in range(5):
            out[X_R + k : X_R + k + 1, :] = parts[1 + k]
        out[X_R + 5 : X_R + 8, :] = jnp.zeros((3, HALF), F32)


def stream(v, x, low, post, zin, ypin, ymin, xpin, xmin, nozzle, wall):
    lane = lanes((SZ_, HALF))
    layer = rows_of((SZ_, HALF))
    a, b, c = VEL[v]
    s = x - a
    inside = 0 <= s < SX
    edge = xpin if s < 0 else xmin
    if inside:
        tiles = [post[v, s, :, HALF * h : HALF * h + HALF] for h in range(2)]
    else:
        n = (X_UP if s < 0 else X_DN).index(v)
        tiles = [edge[32 * n + 16 * h : 32 * n + 16 * h + 16, :] for h in range(2)]
    beside = None
    if b:
        slab = ypin if b > 0 else ymin
        k = 4 * (Y_UP if b > 0 else Y_DN).index(v)
        if inside:
            k, column = k + s, slab[0:16, :]
        else:
            k, column = k + (3 if s < 0 else 0) + (1 if b < 0 else 0), edge[X_T : X_T + 16, :]
        beside = roll(column, (0 if b > 0 else HALF - 1) - k, 1)
    if c:
        n = (Z_UP if c > 0 else Z_DN).index(v)
        at = 0 if c > 0 else SZ_ - 1
        for h in range(2):
            k = 20 * h + 4 * n + s
            row = zin[k : k + 1, :] if inside else edge[X_R + h : X_R + h + 1, :]
            tiles[h] = jnp.where(layer == at, row, roll(tiles[h], c, 0))
        if b:
            corner = roll(slab[Y_D + x : Y_D + x + 1, :], b, 1)
            beside = jnp.where(layer == at, corner, roll(beside, c, 0))
    if b > 0:
        t0, t1 = roll(tiles[0], 1, 1), roll(tiles[1], 1, 1)
        tiles = [jnp.where(lane == 0, beside, t0), jnp.where(lane == 0, t0, t1)]
    elif b < 0:
        t0, t1 = roll(tiles[0], -1, 1), roll(tiles[1], -1, 1)
        tiles = [jnp.where(lane == HALF - 1, t1, t0), jnp.where(lane == HALF - 1, beside, t1)]
    for h in range(2):
        y = slice(HALF * h, HALF * h + HALF)
        if c > 0:
            back = post[OPP[v], x, 0:1, y]
            tiles[h] = jnp.where((layer == 0) & low, back, tiles[h])
        elif c < 0:
            back = post[OPP[v], x, SZ_ - 1 : SZ_, y]
            through = post[v, x, SZ_ - 1 : SZ_, y]
            top = jnp.where(
                nozzle[x : x + 1, y] == 1,
                back + 6.0 * WEIGHT[v] * JET_SPEED,
                jnp.where(wall[x : x + 1, y] == 1, through, back),
            )
            tiles[h] = jnp.where((layer == SZ_ - 1) & jnp.logical_not(low), top, tiles[h])
    return tiles


INNER = tuple(v for v in range(19) if VEL[v][1] == 0)
SIDE = tuple(v for v in range(19) if VEL[v][1] != 0)


def put_inside(velocities, low, out, buf, sems, *state):
    copies = []
    for i, v in enumerate(velocities):
        a = VEL[v][0]
        first, last = max(a, 0), SX + min(a, 0)
        for x in range(first, last):
            for h, tile in enumerate(stream(v, x, low, *state)):
                buf[i, x, :, HALF * h : HALF * h + HALF] = tile
        copy = pltpu.make_async_copy(buf.at[i, first:last], out.at[v, first:last], sems.at[i])
        copy.start()
        copies.append(copy)
    for copy in copies:
        copy.wait()


def inner_kernel(post, zin, nozzle, wall, out, buf, sems):
    low = lax.axis_index("gz") == 0
    put_inside(INNER, low, out, buf, sems, post, zin, None, None, None, None, nozzle, wall)


def side_kernel(whole, post, zin, ypin, ymin, nozzle, wall, out, buf, sems):
    low = lax.axis_index("gz") == 0
    put_inside(SIDE, low, out, buf, sems, post, zin, ypin, ymin, None, None, nozzle, wall)


def spread(folded, at):
    return jnp.concatenate([roll(folded, at - 32 * g, 1) for g in range(4)], axis=0)


def vertical(c):
    down = jnp.where(rows_of((DEPTH, HALF)) == DEPTH - 1, 0.0, 0.5 * (c + roll(c, -1, 0)))
    return down, roll(down, 1, 0)


def around(*links):
    total = None
    for link, value in links:
        total = link * value if total is None else total + link * value
    return total


def beside_of(value, left_col, right_col):
    lane = lanes((DEPTH, HALF))
    return (
        jnp.where(lane == 0, left_col, roll(value, 1, 1)),
        jnp.where(lane == HALF - 1, right_col, roll(value, -1, 1)),
    )


def columns(pair, x):
    at = (4 * x) % HALF
    return roll(pair[0], -at, 1), roll(pair[1], HALF - 1 - at, 1)


def sources(u, load, cool, warm):
    depth = rows_of((DEPTH, HALF))
    floor, face = depth == 0, depth == DEPTH - 1
    base = u + jnp.where(floor, load, 0.0) + jnp.where(face, warm * cool, 0.0)
    return base, 1.0 + jnp.where(face, warm, 0.0)


def sink_kernel(temp, cond, own, misc, zbuf, zin, ypin, ymin, cell, edge):
    low = lax.axis_index("gz") == 0
    lane = lanes((DEPTH, HALF))
    left, right = halo_slabs(low, zin, ypin, ymin)
    own_edges = own[...]
    row_left = jnp.where(low, ypin[Y_E : Y_E + 1, :], zin[Z_E + 4 : Z_E + 5, :])
    row_right = jnp.where(low, zin[Z_E + 4 : Z_E + 5, :], ymin[Y_E : Y_E + 1, :])
    heat_left = jnp.where(low, roll(row_left, -48, 1), roll(row_left, -32, 1))
    heat_right = jnp.where(low, roll(zbuf[Z_E + 4 : Z_E + 5, :], -49, 1), roll(row_right, -33, 1))
    pair_u, pair_c, pair_f = [], [], []
    for side, (folded, j1, j2, jo, row, h_row, jr) in enumerate((
        (left, 1, 0, 2, row_left, heat_left, 0),
        (right, 2, 3, 1, row_right, heat_right, 1),
    )):
        u1, u2 = spread(folded, -j1), spread(folded, -j2)
        c1, c2 = spread(folded, -16 - j1), spread(folded, -16 - j2)
        uo, co = roll(own_edges, -jo, 1), roll(own_edges, -16 - jo, 1)
        g_far, g_own = 0.5 * (c1 + c2), 0.5 * (c1 + co)
        g_up = jnp.where(lane < 12, 0.5 * (c1 + roll(c1, -4, 1)), 0.0)
        g_dn = jnp.where(lane >= 4, roll(g_up, 4, 1), 0.0)
        v_dn, v_up = vertical(c1)
        base, rest = sources(u1, roll(row, -jr, 1), roll(row, -16 - jr, 1), h_row)
        den = rest + (g_far + g_own) + (g_up + g_dn) + (v_dn + v_up)
        num = base + around((g_far, u2), (g_own, uo), (g_up, roll(u1, -4, 1)), (g_dn, roll(u1, 4, 1)),
                            (v_dn, roll(u1, -1, 0)), (v_up, roll(u1, 1, 0)))
        edge[side, 0], edge[side, 1], edge[side, 2], edge[side, 3] = u1, c1, num, den
        pair_u.append(u1)
        pair_c.append(c1)
        pair_f.append(num / den)
    warm = jnp.where(low, misc[8:12, :], zin[Z_E : Z_E + 4, :])
    g_x = {x: 0.5 * (cond[x] + cond[x + 1]) for x in range(SX - 1)}
    first, inverse = {}, {}
    for x in range(SX):
        u, c = temp[x], cond[x]
        c_l, c_r = beside_of(c, *columns(pair_c, x))
        u_l, u_r = beside_of(u, *columns(pair_u, x))
        g_l, g_r = 0.5 * (c + c_l), 0.5 * (c + c_r)
        v_dn, v_up = vertical(c)
        base, den = sources(u, misc[x : x + 1, :], misc[4 + x : 5 + x, :], warm[x : x + 1, :])
        den = den + (g_l + g_r) + (v_dn + v_up)
        num = base + around((g_l, u_l), (g_r, u_r), (v_dn, roll(u, -1, 0)), (v_up, roll(u, 1, 0)))
        if x > 0:
            den, num = den + g_x[x - 1], num + g_x[x - 1] * temp[x - 1]
        if x < SX - 1:
            den, num = den + g_x[x], num + g_x[x] * temp[x + 1]
        for k, value in enumerate((num, den, base, g_l, g_r, v_dn)):
            cell[k, x] = value
        if 0 < x < SX - 1:
            inverse[x] = 1.0 / den
            first[x] = num * inverse[x]
    for x, other in ((1, 2), (2, 1)):
        f = first[x]
        f_l, f_r = beside_of(f, *columns(pair_f, x))
        v_dn = cell[5, x]
        num = cell[2, x] + g_x[1] * first[other] + around(
            (cell[3, x], f_l), (cell[4, x], f_r), (v_dn, roll(f, -1, 0)), (roll(v_dn, 1, 0), roll(f, 1, 0)))
        cell[0, x], cell[1, x], cell[2, x] = f, inverse[x], num


def final_kernel(
    whole, post, zin, ypin, ymin, xa, xb, nozzle, wall, temp, cond, cell, edges,
    pops_out, solid_out, xpin, xmin, buf, solid, sems,
):
    low = lax.axis_index("gz") == 0
    paired = checker()
    xpin[...] = jnp.where(paired, xb[...], xa[...])
    xmin[...] = jnp.where(paired, xa[...], xb[...])
    copies = []
    for i, v in enumerate(X_UP + X_DN):
        x = 0 if i < 5 else SX - 1
        for h, tile in enumerate(stream(v, x, low, post, zin, ypin, ymin, xpin, xmin, nozzle, wall)):
            buf[i, :, HALF * h : HALF * h + HALF] = tile
        copies.append(pltpu.make_async_copy(buf.at[i], pops_out.at[v, x], sems.at[i]))
        copies[-1].start()

    lane = lanes((DEPTH, HALF))
    before, after = xpin[X_T : X_T + 16, :], xmin[X_T : X_T + 16, :]
    pair_u, pair_c, pair_f = [], [], []
    for side, j in ((0, 1), (1, 2)):
        u1, c1 = edges[side, 0], edges[side, 1]
        u1 = jnp.where(lane == 124, spread(before, 112 - j), jnp.where(lane == 16, spread(after, 16 - j), u1))
        c1 = jnp.where(lane == 124, spread(before, 96 - j), jnp.where(lane == 16, spread(after, -j), c1))
        g_up = 0.5 * (c1 + roll(c1, -4, 1))
        g_dn = jnp.where(lane == 0, roll(g_up, 4, 1), 0.0)
        g_up = jnp.where(lane == 12, g_up, 0.0)
        num = edges[side, 2] + around((g_up, roll(u1, -4, 1)), (g_dn, roll(u1, 4, 1)))
        pair_u.append(u1)
        pair_c.append(c1)
        pair_f.append(num / (edges[side, 3] + g_up + g_dn))
    first, inverse, g_x = {1: cell[0, 1], 2: cell[0, 2]}, {1: cell[1, 1], 2: cell[1, 2]}, {}
    for side, x, n, inner in ((xpin, -1, 0, 1), (xmin, 4, 3, 2)):
        u, u_far = side[X_U : X_U + 64, :], side[X_U + 64 : X_U + 128, :]
        c, c_far = side[X_U + 128 : X_U + 192, :], side[X_U + 192 : X_U + 256, :]
        link, g_far = 0.5 * (c + cond[n]), 0.5 * (c + c_far)
        c_l, c_r = beside_of(c, *columns(pair_c, x))
        u_l, u_r = beside_of(u, *columns(pair_u, x))
        g_l, g_r = 0.5 * (c + c_l), 0.5 * (c + c_r)
        v_dn, v_up = vertical(c)
        base, den = sources(u, *(side[X_R + 2 + k : X_R + 3 + k, :] for k in range(3)))
        den = den + (link + g_far) + (g_l + g_r) + (v_dn + v_up)
        num = base + around((g_far, u_far), (link, temp[n]), (g_l, u_l), (g_r, u_r),
                            (v_dn, roll(u, -1, 0)), (v_up, roll(u, 1, 0)))
        outer = num / den
        inverse[n] = 1.0 / (cell[1, n] + link)
        first[n] = (cell[0, n] + link * u) * inverse[n]
        f = first[n]
        f_l, f_r = beside_of(f, *columns(pair_f, n))
        v_dn = cell[5, n]
        g_x[inner] = 0.5 * (cond[n] + cond[inner])
        num = cell[2, n] + link * outer + g_x[inner] * first[inner] + around(
            (cell[3, n], f_l), (cell[4, n], f_r), (v_dn, roll(f, -1, 0)), (roll(v_dn, 1, 0), roll(f, 1, 0)))
        solid[n] = num * inverse[n]
        solid[inner] = (cell[2, inner] + g_x[inner] * f) * inverse[inner]
        for k in (n, inner):
            copies.append(pltpu.make_async_copy(solid.at[k], solid_out.at[k], sems.at[10 + k]))
            copies[-1].start()
    for copy in copies:
        copy.wait()


def shape(*dims):
    return pltpu.HBM(dims, F32)


def near(*dims):
    return pltpu.VMEM(dims, F32)


def hold(array, kind):
    return pltpu.with_memory_space_constraint(array, pltpu.VMEM if kind == "near" else pltpu.HBM)


VM = pl.BlockSpec(memory_space=pltpu.VMEM)
ANY = pl.BlockSpec(memory_space=pl.ANY)


def ring(axis, step):
    n = lax.axis_size(axis)
    return [(i, (i + step) % n) for i in range(n)]


def pairs(axis, odd):
    n = lax.axis_size(axis)
    return [(i, (i + 1) % n if i % 2 == odd else (i - 1) % n) for i in range(n)]


def checker_pairs(turn):
    ny, nz = lax.axis_size("gy"), lax.axis_size("gz")
    return [
        ((i * ny + y) * nz + z, (j * ny + y) * nz + z)
        for y in range(ny) for i, j in pairs("gx", (int(odd_first(y)) + turn) % 2) for z in range(nz)
    ]


def call(kernel, name, inputs, outputs, scratch=(), aliases=None):
    spaces = [ANY if kind == "far" else VM for kind, _ in inputs]
    arrays = [hold(a, kind) for kind, a in inputs]
    return pl.pallas_call(
        kernel,
        name=name,
        in_specs=spaces,
        out_specs=[ANY if o.memory_space == pltpu.HBM else VM for o in outputs],
        out_shape=list(outputs),
        scratch_shapes=list(scratch),
        input_output_aliases=aliases or {},
        compiler_params=pltpu.CompilerParams(vmem_limit_bytes=16 * 1024 * 1024),
    )(*arrays)


def far(*arrays):
    return [("far", a) for a in arrays]


def kept(*arrays):
    return [("near", a) for a in arrays]


def body(populations, nozzle_mask, wall_type, solid_temp, diffusion, heat_load, coolant_temp):
    dma = pltpu.SemaphoreType.DMA
    zbuf, own, misc, temp, cond = call(
        face_kernel, "face",
        far(populations, solid_temp, diffusion, heat_load, coolant_temp),
        [near(Z_ROWS, HALF), near(DEPTH, HALF), near(16, HALF), near(SX, DEPTH, HALF), near(SX, DEPTH, HALF)],
        [pltpu.VMEM((2, 19, 8, HALF), F32), dma((8,))],
    )
    zin = lax.ppermute(zbuf, "gz", ring("gz", 1))
    post, yp, ym, xa, xb, nozzle, wall = call(
        collide_kernel, "collide",
        far(populations, nozzle_mask, wall_type) + kept(temp, cond),
        [near(19, SX, SZ_, 2 * HALF), near(16, HALF), near(16, HALF), near(X_ROWS, HALF), near(X_ROWS, HALF),
         pltpu.VMEM((SX, 2 * HALF), jnp.int32), pltpu.VMEM((SX, 2 * HALF), jnp.int32)],
        [pltpu.VMEM((19, SX, SZ_, 2 * HALF), F32), pltpu.VMEM((X_U, HALF), F32), dma((SX + 2,))],
    )
    yao, ybo = call(y_kernel, "pack_y", kept(yp, ym, zbuf, zin), [near(Y_ROWS, HALF)] * 2)
    ya = lax.ppermute(yao, "gy", pairs("gy", 0))
    yb = lax.ppermute(ybo, "gy", pairs("gy", 1))
    (pops,) = call(
        inner_kernel, "inner", kept(post, zin, nozzle, wall), [shape(19, SX, SZ_, 2 * HALF)],
        [pltpu.VMEM((len(INNER), SX, SZ_, 2 * HALF), F32), dma((len(INNER),))],
    )
    xao, xbo, ypin, ymin = call(
        x_kernel, "pack_x", kept(xa, xb, zin, ya, yb, misc) + far(pops),
        [near(X_ROWS, HALF)] * 2 + [near(Y_ROWS, HALF)] * 2, aliases={0: 0, 1: 1},
    )
    xa = lax.ppermute(xao, ("gx", "gy", "gz"), checker_pairs(0))
    xb = lax.ppermute(xbo, ("gx", "gy", "gz"), checker_pairs(1))
    cell, edge = call(
        sink_kernel, "sink", kept(temp, cond, own, misc, zbuf, zin, ypin, ymin),
        [near(6, SX, DEPTH, HALF), near(2, 4, DEPTH, HALF)],
    )
    (pops,) = call(
        side_kernel, "side", far(pops) + kept(post, zin, ypin, ymin, nozzle, wall), [shape(19, SX, SZ_, 2 * HALF)],
        [pltpu.VMEM((len(SIDE), SX, SZ_, 2 * HALF), F32), dma((len(SIDE),))], {0: 0},
    )
    return tuple(call(
        final_kernel, "finish",
        far(pops) + kept(post, zin, ypin, ymin, xa, xb, nozzle, wall, temp, cond, cell, edge),
        [shape(19, SX, SZ_, 2 * HALF), shape(SX, DEPTH, HALF)],
        [pltpu.VMEM((X_ROWS, HALF), F32), pltpu.VMEM((X_ROWS, HALF), F32),
         pltpu.VMEM((10, SZ_, 2 * HALF), F32), pltpu.VMEM((SX, DEPTH, HALF), F32), dma((14,))], {0: 0},
    ))


def solution(mesh):
    placed = (
        P(None, "gx", "gz", "gy"),
        P("gx", "gy"),
        P("gx", "gy"),
        P("gx", None, ("gy", "gz")),
        P("gx", None, ("gy", "gz")),
        P("gx", ("gy", "gz")),
        P("gx", ("gy", "gz")),
    )
    return jax.shard_map(
        body,
        mesh=mesh,
        in_specs=placed,
        out_specs=(P(None, "gx", "gz", "gy"), P("gx", None, ("gy", "gz"))),
        check_vma=False,
    )
```

```python
import jax
import jax.numpy as jnp
from jax import lax
from jax.experimental import pallas as pl
from jax.experimental.pallas import tpu as pltpu
from jax.sharding import PartitionSpec as P

F32 = jnp.float32
JET_SPEED = 0.1
H_BASE = 0.5
H_GAIN = 40.0
SHEAR_RATE = 1.6
ODD_RATE = 1.2
EVEN_RATE = 1.4
VEL = (
    (0, 0, 0),
    (1, 0, 0), (-1, 0, 0), (0, 1, 0), (0, -1, 0), (0, 0, 1), (0, 0, -1),
    (1, 1, 0), (-1, -1, 0), (1, -1, 0), (-1, 1, 0),
    (1, 0, 1), (-1, 0, -1), (1, 0, -1), (-1, 0, 1),
    (0, 1, 1), (0, -1, -1), (0, 1, -1), (0, -1, 1),
)
OPP = tuple(VEL.index(tuple(-e for e in v)) for v in VEL)
WEIGHT = (1.0 / 3.0,) + (1.0 / 18.0,) * 6 + (1.0 / 36.0,) * 12
X_UP, X_DN = (1, 7, 9, 11, 13), (2, 10, 8, 14, 12)
Y_UP, Y_DN = (3, 7, 10, 15, 17), (4, 9, 8, 18, 16)
Z_UP, Z_DN = (5, 11, 14, 15, 18), (6, 13, 12, 17, 16)
SX, SZ_, HALF = 4, 16, 128
DEPTH = 64
Z_S, Z_E, Z_ROWS = 40, 56, 64
Y_S, Y_E, Y_D, Y_ROWS = 16, 32, 40, 48
X_U, X_T, X_R, X_ROWS = 160, 416, 432, 440


def roll(value, shift, axis):
    size = value.shape[axis]
    shift = shift % size
    return value if shift == 0 else pltpu.roll(value, shift, axis)


def lanes(shape):
    return lax.broadcasted_iota(jnp.int32, shape, len(shape) - 1)


def rows_of(shape):
    return lax.broadcasted_iota(jnp.int32, shape, 0)


def collide(f):
    s = {i: f[i] + f[i + 1] for i in range(1, 19, 2)}
    d = {i: f[i] - f[i + 1] for i in range(1, 19, 2)}
    s_ab, s_ac, s_bc = s[7] + s[9], s[11] + s[13], s[15] + s[17]
    rho = (f[0] + s[1]) + (s[3] + s[5]) + (s_ab + s_ac + s_bc)
    m_a = d[1] + (d[7] + d[9]) + (d[11] + d[13])
    m_b = d[3] + (d[7] - d[9]) + (d[15] + d[17])
    m_c = d[5] + (d[11] - d[13]) + (d[15] - d[17])
    inv = 1.0 / rho
    u_a, u_b, u_c = m_a * inv, m_b * inv, m_c * inv
    p_aa, p_bb, p_cc = m_a * u_a, m_b * u_b, m_c * u_c
    p_ab, p_ac, p_bc = m_a * u_b, m_a * u_c, m_b * u_c
    q = p_aa + p_bb + p_cc
    base = rho - 1.5 * q
    t = rho - 2.0 * q
    t_ab = 4.0 * f[0] - 2.0 * (s[1] + s[3]) + s_ab - (t + 0.5 * p_cc)
    t_ac = 4.0 * f[0] - 2.0 * (s[1] + s[5]) + s_ac - (t + 0.5 * p_bb)
    t_bc = 4.0 * f[0] - 2.0 * (s[3] + s[5]) + s_bc - (t + 0.5 * p_aa)
    mean = (2.0 / 7.0) * (t_ab + t_ac + t_bc)
    gain = (SHEAR_RATE - EVEN_RATE) / 12.0
    c_ab, c_ac, c_bc = gain * (t_ab - mean), gain * (t_ac - mean), gain * (t_bc - mean)
    keep, half_keep, half = 1.0 - SHEAR_RATE, 0.5 * (1.0 - SHEAR_RATE), 0.5 * SHEAR_RATE
    odd, pull = 0.5 * (1.0 - ODD_RATE), 3.0 * ODD_RATE
    post = [None] * 19
    post[0] = keep * f[0] + (SHEAR_RATE / 3.0) * base + 4.0 * (c_ab + c_ac + c_bc)

    def put(i, extra, equil, moment, weight):
        even = half_keep * s[i] + equil + extra
        anti = odd * d[i] + (pull * weight) * moment
        post[i] = even + anti
        post[i + 1] = even - anti

    axis = half / 9.0
    for i, p, c, m in ((1, p_aa, c_ab + c_ac, m_a), (3, p_bb, c_ab + c_bc, m_b), (5, p_cc, c_ac + c_bc, m_c)):
        put(i, -2.0 * c, axis * (base + 4.5 * p), m, 1.0 / 18.0)
    diag = half / 18.0
    for i, pp, pq, c, m, n in (
        (7, p_aa + p_bb, p_ab, c_ab, m_a, m_b),
        (11, p_aa + p_cc, p_ac, c_ac, m_a, m_c),
        (15, p_bb + p_cc, p_bc, c_bc, m_b, m_c),
    ):
        even = diag * (base + 4.5 * pp)
        cross = (9.0 * diag) * pq
        put(i, c, even + cross, m + n, 1.0 / 36.0)
        put(i + 2, c, even - cross, m - n, 1.0 / 36.0)
    return post, q * inv


def even(axis):
    return (lax.axis_index(axis) & 1) == 0


def odd_first(y):
    return (y < 2) | (y % 2 == 0)


def checker():
    odd = odd_first(lax.axis_index("gy"))
    return (lax.axis_index("gx") & 1) == jnp.where(odd, 1, 0)


def face_kernel(pops, temp, cond, load, cool, zbuf, own, misc, tempv, condv, popsv, buf, sems):
    low = lax.axis_index("gz") == 0
    face = jnp.where(low, SZ_ - 1, 0)
    fields = [
        pltpu.make_async_copy(temp, tempv, sems.at[0]),
        pltpu.make_async_copy(cond, condv, sems.at[1]),
        pltpu.make_async_copy(load, misc.at[0:4], sems.at[2]),
        pltpu.make_async_copy(cool, misc.at[4:8], sems.at[3]),
    ]
    rows = [
        [
            pltpu.make_async_copy(
                pops.at[:, :, layer, HALF * h : HALF * h + HALF],
                buf.at[k, :, 4 * h : 4 * h + 4, :],
                sems.at[4 + 2 * k + h],
            )
            for h in range(2)
        ]
        for k, layer in enumerate((face, 0))
    ]
    for copy in rows[0] + fields:
        copy.start()
    whole = pltpu.make_async_copy(pops, popsv, sems.at[8])
    whole.start()

    @pl.when(low)
    def _():
        for copy in rows[1]:
            copy.start()

    for copy in fields:
        copy.wait()
    lane = lanes((DEPTH, HALF))
    edges = jnp.zeros((DEPTH, HALF), F32)
    for k, field in enumerate((tempv, condv)):
        for x in range(SX):
            at = k * 16 + x * 4
            edges = jnp.where((lane >= at) & (lane < at + 4), roll(field[x], at + 2, 1), edges)
    own[...] = edges
    lane16 = lanes((16, HALF))
    fold = edges[0:16]
    for g in range(1, 4):
        fold = jnp.where(lane16 >= 32 * g, roll(edges[16 * g : 16 * g + 16], 32 * g, 1), fold)
    zbuf[Z_S : Z_S + 16, :] = fold
    for copy in rows[0]:
        copy.wait()
    out, _ = collide([buf[0, v] for v in range(19)])
    for n in range(5):
        leaving = jnp.where(low, out[Z_UP[n]], out[Z_DN[n]])
        for h in range(2):
            zbuf[20 * h + 4 * n : 20 * h + 4 * n + 4, :] = leaving[4 * h : 4 * h + 4, :]
    misc[8:16, :] = jnp.zeros((8, HALF), F32)

    @pl.when(low)
    def _():
        for copy in rows[1]:
            copy.wait()
        _, speed = collide([buf[1, v] for v in range(19)])
        misc[8:16, :] = H_BASE + H_GAIN * speed

    lane1 = lanes((1, HALF))
    row = jnp.zeros((1, HALF), F32)
    for k in range(4):
        for x in range(SX):
            at = k * 16 + x * 4
            value = misc[4 * k + x : 4 * k + x + 1, :]
            row = jnp.where((lane1 >= at) & (lane1 < at + 2), roll(value, at + 1, 1), row)
    zbuf[Z_E : Z_E + 4, :] = misc[12:16, :]
    zbuf[Z_E + 4 : Z_E + 5, :] = row
    zbuf[Z_E + 5 : Z_E + 8, :] = jnp.zeros((3, HALF), F32)
    whole.wait()


def collide_kernel(nozzle, wall, buf, tempv, condv, post, yp, ym, xa, xb, nozzlev, wallv, face, sems):
    plates = [
        pltpu.make_async_copy(nozzle, nozzlev, sems.at[0]),
        pltpu.make_async_copy(wall, wallv, sems.at[1]),
    ]
    for copy in plates:
        copy.start()
    paired = checker()
    for k, field in enumerate((tempv, condv)):
        for j in range(2):
            at = X_U + 128 * k + 64 * j
            up, dn = field[3 - j], field[j]
            xa[at : at + 64, :] = jnp.where(paired, up, dn)
            xb[at : at + 64, :] = jnp.where(paired, dn, up)
    y_up = [jnp.zeros((8, HALF), F32) for _ in range(2)]
    y_dn = [jnp.zeros((8, HALF), F32) for _ in range(2)]
    lane8 = lanes((8, HALF))
    for x in range(SX):
        for k in range(2):
            z = slice(8 * k, 8 * k + 8)
            for h in range(2):
                y = slice(HALF * h, HALF * h + HALF)
                out, _ = collide([buf[v, x, z, y] for v in range(19)])
                for v in range(19):
                    post[v, x, z, y] = out[v]
                for n in range(5):
                    at = 4 * n + x
                    if h == 1:
                        y_up[k] = jnp.where(lane8 == at, roll(out[Y_UP[n]], at - 127, 1), y_up[k])
                    else:
                        y_dn[k] = jnp.where(lane8 == at, roll(out[Y_DN[n]], at, 1), y_dn[k])
                    at = 32 * n + 16 * h + 8 * k
                    if x == 3:
                        up, dn = out[X_UP[n]], face[at : at + 8, :]
                        xa[at : at + 8, :] = jnp.where(paired, up, dn)
                        xb[at : at + 8, :] = jnp.where(paired, dn, up)
                    if x == 0:
                        face[at : at + 8, :] = out[X_DN[n]]
    for k in range(2):
        yp[8 * k : 8 * k + 8, :] = y_up[k]
        ym[8 * k : 8 * k + 8, :] = y_dn[k]
    for copy in plates:
        copy.wait()


def y_kernel(yp, ym, zbuf, zin, outa, outb):
    low = lax.axis_index("gz") == 0
    paired = even("gy")
    lane = lanes((1, HALF))
    sent = zin[Z_E + 4 : Z_E + 5, :]
    row = jnp.where((lane >= 32) & low, zbuf[Z_E + 4 : Z_E + 5, :], sent)
    up, dn = yp[...], ym[...]
    c_up, c_dn = zin[32:36, :], zin[16:20, :]
    for out, own_up in ((outa, paired), (outb, jnp.logical_not(paired))):
        out[0:16, :] = jnp.where(own_up, up, dn)
        out[Y_S : Y_S + 16, :] = zin[Z_S : Z_S + 16, :]
        out[Y_E : Y_E + 8, :] = jnp.broadcast_to(row, (8, HALF))
        out[Y_D : Y_D + 4, :] = jnp.where(own_up, c_up, c_dn)
        out[Y_D + 4 : Y_D + 8, :] = jnp.zeros((4, HALF), F32)


def halo_slabs(low, zin, ypin, ymin):
    left = jnp.where(low, ypin[Y_S : Y_S + 16, :], zin[Z_S : Z_S + 16, :])
    right = jnp.where(low, zin[Z_S : Z_S + 16, :], ymin[Y_S : Y_S + 16, :])
    return left, right


def x_kernel(ina, inb, zin, ya, yb, misc, pops, outa, outb, ypin, ymin):
    low = lax.axis_index("gz") == 0
    paired = even("gy")
    ypin[...] = jnp.where(paired, yb[...], ya[...])
    ymin[...] = jnp.where(paired, ya[...], yb[...])
    left, right = halo_slabs(low, zin, ypin, ymin)
    warm = jnp.where(low, misc[8:12, :], zin[Z_E : Z_E + 4, :])
    lane = lanes((16, HALF))
    tails = []
    for x, n, up, dn in ((3, 1, 7, 9), (0, 2, 10, 8)):
        k_up, k_dn = 4 * Y_UP.index(up) + x, 4 * Y_DN.index(dn) + x + 1
        slab = jnp.where((lane & 15) == 4 * x + 1, left, right)
        slab = jnp.where(lane == k_up, ypin[0:16, :], slab)
        slab = jnp.where(lane == k_dn, roll(ymin[0:16, :], 1, 1), slab)
        at = 4 * n + x
        tails.append((slab, zin[at : at + 1, :], zin[20 + at : 21 + at, :],
                      misc[x : x + 1, :], misc[4 + x : 5 + x, :], warm[x : x + 1, :]))
    paired = checker()
    for out, (first, second) in ((outa, (0, 1)), (outb, (1, 0))):
        parts = [jnp.where(paired, u, v) for u, v in zip(tails[first], tails[second])]
        out[X_T : X_T + 16, :] = parts[0]
        for k in range(5):
            out[X_R + k : X_R + k + 1, :] = parts[1 + k]
        out[X_R + 5 : X_R + 8, :] = jnp.zeros((3, HALF), F32)


def stream(v, x, low, post, zin, ypin, ymin, xpin, xmin, nozzle, wall):
    lane = lanes((SZ_, HALF))
    layer = rows_of((SZ_, HALF))
    a, b, c = VEL[v]
    s = x - a
    inside = 0 <= s < SX
    edge = xpin if s < 0 else xmin
    if inside:
        tiles = [post[v, s, :, HALF * h : HALF * h + HALF] for h in range(2)]
    else:
        n = (X_UP if s < 0 else X_DN).index(v)
        tiles = [edge[32 * n + 16 * h : 32 * n + 16 * h + 16, :] for h in range(2)]
    beside = None
    if b:
        slab = ypin if b > 0 else ymin
        k = 4 * (Y_UP if b > 0 else Y_DN).index(v)
        if inside:
            k, column = k + s, slab[0:16, :]
        else:
            k, column = k + (3 if s < 0 else 0) + (1 if b < 0 else 0), edge[X_T : X_T + 16, :]
        beside = roll(column, (0 if b > 0 else HALF - 1) - k, 1)
    if c:
        n = (Z_UP if c > 0 else Z_DN).index(v)
        at = 0 if c > 0 else SZ_ - 1
        for h in range(2):
            k = 20 * h + 4 * n + s
            row = zin[k : k + 1, :] if inside else edge[X_R + h : X_R + h + 1, :]
            tiles[h] = jnp.where(layer == at, row, roll(tiles[h], c, 0))
        if b:
            corner = roll(slab[Y_D + x : Y_D + x + 1, :], b, 1)
            beside = jnp.where(layer == at, corner, roll(beside, c, 0))
    if b > 0:
        t0, t1 = roll(tiles[0], 1, 1), roll(tiles[1], 1, 1)
        tiles = [jnp.where(lane == 0, beside, t0), jnp.where(lane == 0, t0, t1)]
    elif b < 0:
        t0, t1 = roll(tiles[0], -1, 1), roll(tiles[1], -1, 1)
        tiles = [jnp.where(lane == HALF - 1, t1, t0), jnp.where(lane == HALF - 1, beside, t1)]
    for h in range(2):
        y = slice(HALF * h, HALF * h + HALF)
        if c > 0:
            back = post[OPP[v], x, 0:1, y]
            tiles[h] = jnp.where((layer == 0) & low, back, tiles[h])
        elif c < 0:
            back = post[OPP[v], x, SZ_ - 1 : SZ_, y]
            through = post[v, x, SZ_ - 1 : SZ_, y]
            top = jnp.where(
                nozzle[x : x + 1, y] == 1,
                back + 6.0 * WEIGHT[v] * JET_SPEED,
                jnp.where(wall[x : x + 1, y] == 1, through, back),
            )
            tiles[h] = jnp.where((layer == SZ_ - 1) & jnp.logical_not(low), top, tiles[h])
    return tiles


INNER = tuple(v for v in range(19) if VEL[v][1] == 0)
SIDE = tuple(v for v in range(19) if VEL[v][1] != 0)


def put_inside(velocities, low, out, buf, sems, *state):
    copies = []
    for i, v in enumerate(velocities):
        a = VEL[v][0]
        first, last = max(a, 0), SX + min(a, 0)
        for x in range(first, last):
            for h, tile in enumerate(stream(v, x, low, *state)):
                buf[i, x, :, HALF * h : HALF * h + HALF] = tile
        copy = pltpu.make_async_copy(buf.at[i, first:last], out.at[v, first:last], sems.at[i])
        copy.start()
        copies.append(copy)
    for copy in copies:
        copy.wait()


def inner_kernel(post, zin, nozzle, wall, out, buf, sems):
    low = lax.axis_index("gz") == 0
    put_inside(INNER, low, out, buf, sems, post, zin, None, None, None, None, nozzle, wall)


def side_kernel(whole, post, zin, ypin, ymin, nozzle, wall, out, buf, sems):
    low = lax.axis_index("gz") == 0
    put_inside(SIDE, low, out, buf, sems, post, zin, ypin, ymin, None, None, nozzle, wall)


def spread(folded, at):
    return jnp.concatenate([roll(folded, at - 32 * g, 1) for g in range(4)], axis=0)


def vertical(c):
    down = jnp.where(rows_of((DEPTH, HALF)) == DEPTH - 1, 0.0, 0.5 * (c + roll(c, -1, 0)))
    return down, roll(down, 1, 0)


def around(*links):
    total = None
    for link, value in links:
        total = link * value if total is None else total + link * value
    return total


def beside_of(value, left_col, right_col):
    lane = lanes((DEPTH, HALF))
    return (
        jnp.where(lane == 0, left_col, roll(value, 1, 1)),
        jnp.where(lane == HALF - 1, right_col, roll(value, -1, 1)),
    )


def columns(pair, x):
    at = (4 * x) % HALF
    return roll(pair[0], -at, 1), roll(pair[1], HALF - 1 - at, 1)


def sources(u, load, cool, warm):
    depth = rows_of((DEPTH, HALF))
    floor, face = depth == 0, depth == DEPTH - 1
    base = u + jnp.where(floor, load, 0.0) + jnp.where(face, warm * cool, 0.0)
    return base, 1.0 + jnp.where(face, warm, 0.0)


def sink_kernel(temp, cond, own, misc, zbuf, zin, ypin, ymin, cell, edge):
    low = lax.axis_index("gz") == 0
    lane = lanes((DEPTH, HALF))
    left, right = halo_slabs(low, zin, ypin, ymin)
    own_edges = own[...]
    row_left = jnp.where(low, ypin[Y_E : Y_E + 1, :], zin[Z_E + 4 : Z_E + 5, :])
    row_right = jnp.where(low, zin[Z_E + 4 : Z_E + 5, :], ymin[Y_E : Y_E + 1, :])
    heat_left = jnp.where(low, roll(row_left, -48, 1), roll(row_left, -32, 1))
    heat_right = jnp.where(low, roll(zbuf[Z_E + 4 : Z_E + 5, :], -49, 1), roll(row_right, -33, 1))
    pair_u, pair_c, pair_f = [], [], []
    for side, (folded, j1, j2, jo, row, h_row, jr) in enumerate((
        (left, 1, 0, 2, row_left, heat_left, 0),
        (right, 2, 3, 1, row_right, heat_right, 1),
    )):
        u1, u2 = spread(folded, -j1), spread(folded, -j2)
        c1, c2 = spread(folded, -16 - j1), spread(folded, -16 - j2)
        uo, co = roll(own_edges, -jo, 1), roll(own_edges, -16 - jo, 1)
        g_far, g_own = 0.5 * (c1 + c2), 0.5 * (c1 + co)
        g_up = jnp.where(lane < 12, 0.5 * (c1 + roll(c1, -4, 1)), 0.0)
        g_dn = jnp.where(lane >= 4, roll(g_up, 4, 1), 0.0)
        v_dn, v_up = vertical(c1)
        base, rest = sources(u1, roll(row, -jr, 1), roll(row, -16 - jr, 1), h_row)
        den = rest + (g_far + g_own) + (g_up + g_dn) + (v_dn + v_up)
        num = base + around((g_far, u2), (g_own, uo), (g_up, roll(u1, -4, 1)), (g_dn, roll(u1, 4, 1)),
                            (v_dn, roll(u1, -1, 0)), (v_up, roll(u1, 1, 0)))
        edge[side, 0], edge[side, 1], edge[side, 2], edge[side, 3] = u1, c1, num, den
        pair_u.append(u1)
        pair_c.append(c1)
        pair_f.append(num / den)
    warm = jnp.where(low, misc[8:12, :], zin[Z_E : Z_E + 4, :])
    g_x = {x: 0.5 * (cond[x] + cond[x + 1]) for x in range(SX - 1)}
    first, inverse = {}, {}
    for x in range(SX):
        u, c = temp[x], cond[x]
        c_l, c_r = beside_of(c, *columns(pair_c, x))
        u_l, u_r = beside_of(u, *columns(pair_u, x))
        g_l, g_r = 0.5 * (c + c_l), 0.5 * (c + c_r)
        v_dn, v_up = vertical(c)
        base, den = sources(u, misc[x : x + 1, :], misc[4 + x : 5 + x, :], warm[x : x + 1, :])
        den = den + (g_l + g_r) + (v_dn + v_up)
        num = base + around((g_l, u_l), (g_r, u_r), (v_dn, roll(u, -1, 0)), (v_up, roll(u, 1, 0)))
        if x > 0:
            den, num = den + g_x[x - 1], num + g_x[x - 1] * temp[x - 1]
        if x < SX - 1:
            den, num = den + g_x[x], num + g_x[x] * temp[x + 1]
        for k, value in enumerate((num, den, base, g_l, g_r, v_dn)):
            cell[k, x] = value
        if 0 < x < SX - 1:
            inverse[x] = 1.0 / den
            first[x] = num * inverse[x]
    for x, other in ((1, 2), (2, 1)):
        f = first[x]
        f_l, f_r = beside_of(f, *columns(pair_f, x))
        v_dn = cell[5, x]
        num = cell[2, x] + g_x[1] * first[other] + around(
            (cell[3, x], f_l), (cell[4, x], f_r), (v_dn, roll(f, -1, 0)), (roll(v_dn, 1, 0), roll(f, 1, 0)))
        cell[0, x], cell[1, x], cell[2, x] = f, inverse[x], num


def final_kernel(
    whole, post, zin, ypin, ymin, xa, xb, nozzle, wall, temp, cond, cell, edges,
    pops_out, solid_out, xpin, xmin, buf, solid, sems,
):
    low = lax.axis_index("gz") == 0
    paired = checker()
    xpin[...] = jnp.where(paired, xb[...], xa[...])
    xmin[...] = jnp.where(paired, xa[...], xb[...])
    copies = []
    for i, v in enumerate(X_UP + X_DN):
        x = 0 if i < 5 else SX - 1
        for h, tile in enumerate(stream(v, x, low, post, zin, ypin, ymin, xpin, xmin, nozzle, wall)):
            buf[i, :, HALF * h : HALF * h + HALF] = tile
        copies.append(pltpu.make_async_copy(buf.at[i], pops_out.at[v, x], sems.at[i]))
        copies[-1].start()

    lane = lanes((DEPTH, HALF))
    before, after = xpin[X_T : X_T + 16, :], xmin[X_T : X_T + 16, :]
    pair_u, pair_c, pair_f = [], [], []
    for side, j in ((0, 1), (1, 2)):
        u1, c1 = edges[side, 0], edges[side, 1]
        u1 = jnp.where(lane == 124, spread(before, 112 - j), jnp.where(lane == 16, spread(after, 16 - j), u1))
        c1 = jnp.where(lane == 124, spread(before, 96 - j), jnp.where(lane == 16, spread(after, -j), c1))
        g_up = 0.5 * (c1 + roll(c1, -4, 1))
        g_dn = jnp.where(lane == 0, roll(g_up, 4, 1), 0.0)
        g_up = jnp.where(lane == 12, g_up, 0.0)
        num = edges[side, 2] + around((g_up, roll(u1, -4, 1)), (g_dn, roll(u1, 4, 1)))
        pair_u.append(u1)
        pair_c.append(c1)
        pair_f.append(num / (edges[side, 3] + g_up + g_dn))
    first, inverse, g_x = {1: cell[0, 1], 2: cell[0, 2]}, {1: cell[1, 1], 2: cell[1, 2]}, {}
    for side, x, n, inner in ((xpin, -1, 0, 1), (xmin, 4, 3, 2)):
        u, u_far = side[X_U : X_U + 64, :], side[X_U + 64 : X_U + 128, :]
        c, c_far = side[X_U + 128 : X_U + 192, :], side[X_U + 192 : X_U + 256, :]
        link, g_far = 0.5 * (c + cond[n]), 0.5 * (c + c_far)
        c_l, c_r = beside_of(c, *columns(pair_c, x))
        u_l, u_r = beside_of(u, *columns(pair_u, x))
        g_l, g_r = 0.5 * (c + c_l), 0.5 * (c + c_r)
        v_dn, v_up = vertical(c)
        base, den = sources(u, *(side[X_R + 2 + k : X_R + 3 + k, :] for k in range(3)))
        den = den + (link + g_far) + (g_l + g_r) + (v_dn + v_up)
        num = base + around((g_far, u_far), (link, temp[n]), (g_l, u_l), (g_r, u_r),
                            (v_dn, roll(u, -1, 0)), (v_up, roll(u, 1, 0)))
        outer = num / den
        inverse[n] = 1.0 / (cell[1, n] + link)
        first[n] = (cell[0, n] + link * u) * inverse[n]
        f = first[n]
        f_l, f_r = beside_of(f, *columns(pair_f, n))
        v_dn = cell[5, n]
        g_x[inner] = 0.5 * (cond[n] + cond[inner])
        num = cell[2, n] + link * outer + g_x[inner] * first[inner] + around(
            (cell[3, n], f_l), (cell[4, n], f_r), (v_dn, roll(f, -1, 0)), (roll(v_dn, 1, 0), roll(f, 1, 0)))
        solid[n] = num * inverse[n]
        solid[inner] = (cell[2, inner] + g_x[inner] * f) * inverse[inner]
        for k in (n, inner):
            copies.append(pltpu.make_async_copy(solid.at[k], solid_out.at[k], sems.at[10 + k]))
            copies[-1].start()
    for copy in copies:
        copy.wait()


def shape(*dims):
    return pltpu.HBM(dims, F32)


def near(*dims):
    return pltpu.VMEM(dims, F32)


def hold(array, kind):
    return pltpu.with_memory_space_constraint(array, pltpu.VMEM if kind == "near" else pltpu.HBM)


VM = pl.BlockSpec(memory_space=pltpu.VMEM)
ANY = pl.BlockSpec(memory_space=pl.ANY)


def ring(axis, step):
    n = lax.axis_size(axis)
    return [(i, (i + step) % n) for i in range(n)]


def pairs(axis, odd):
    n = lax.axis_size(axis)
    return [(i, (i + 1) % n if i % 2 == odd else (i - 1) % n) for i in range(n)]


def checker_pairs(turn):
    ny, nz = lax.axis_size("gy"), lax.axis_size("gz")
    return [
        ((i * ny + y) * nz + z, (j * ny + y) * nz + z)
        for y in range(ny) for i, j in pairs("gx", (int(odd_first(y)) + turn) % 2) for z in range(nz)
    ]


def call(kernel, name, inputs, outputs, scratch=(), aliases=None):
    spaces = [ANY if kind == "far" else VM for kind, _ in inputs]
    arrays = [hold(a, kind) for kind, a in inputs]
    return pl.pallas_call(
        kernel,
        name=name,
        in_specs=spaces,
        out_specs=[ANY if o.memory_space == pltpu.HBM else VM for o in outputs],
        out_shape=list(outputs),
        scratch_shapes=list(scratch),
        input_output_aliases=aliases or {},
        compiler_params=pltpu.CompilerParams(vmem_limit_bytes=16 * 1024 * 1024),
    )(*arrays)


def far(*arrays):
    return [("far", a) for a in arrays]


def kept(*arrays):
    return [("near", a) for a in arrays]


def body(populations, nozzle_mask, wall_type, solid_temp, diffusion, heat_load, coolant_temp):
    dma = pltpu.SemaphoreType.DMA
    zbuf, own, misc, temp, cond, held = call(
        face_kernel, "face",
        far(populations, solid_temp, diffusion, heat_load, coolant_temp),
        [near(Z_ROWS, HALF), near(DEPTH, HALF), near(16, HALF), near(SX, DEPTH, HALF), near(SX, DEPTH, HALF),
         near(19, SX, SZ_, 2 * HALF)],
        [pltpu.VMEM((2, 19, 8, HALF), F32), dma((9,))],
    )
    zin = lax.ppermute(zbuf, "gz", ring("gz", 1))
    post, yp, ym, xa, xb, nozzle, wall = call(
        collide_kernel, "collide",
        far(nozzle_mask, wall_type) + kept(held, temp, cond),
        [near(19, SX, SZ_, 2 * HALF), near(16, HALF), near(16, HALF), near(X_ROWS, HALF), near(X_ROWS, HALF),
         pltpu.VMEM((SX, 2 * HALF), jnp.int32), pltpu.VMEM((SX, 2 * HALF), jnp.int32)],
        [pltpu.VMEM((X_U, HALF), F32), dma((2,))],
    )
    yao, ybo = call(y_kernel, "pack_y", kept(yp, ym, zbuf, zin), [near(Y_ROWS, HALF)] * 2)
    ya = lax.ppermute(yao, "gy", pairs("gy", 0))
    yb = lax.ppermute(ybo, "gy", pairs("gy", 1))
    (pops,) = call(
        inner_kernel, "inner", kept(post, zin, nozzle, wall), [shape(19, SX, SZ_, 2 * HALF)],
        [pltpu.VMEM((len(INNER), SX, SZ_, 2 * HALF), F32), dma((len(INNER),))],
    )
    xao, xbo, ypin, ymin = call(
        x_kernel, "pack_x", kept(xa, xb, zin, ya, yb, misc) + far(pops),
        [near(X_ROWS, HALF)] * 2 + [near(Y_ROWS, HALF)] * 2, aliases={0: 0, 1: 1},
    )
    xa = lax.ppermute(xao, ("gx", "gy", "gz"), checker_pairs(0))
    xb = lax.ppermute(xbo, ("gx", "gy", "gz"), checker_pairs(1))
    cell, edge = call(
        sink_kernel, "sink", kept(temp, cond, own, misc, zbuf, zin, ypin, ymin),
        [near(6, SX, DEPTH, HALF), near(2, 4, DEPTH, HALF)],
    )
    (pops,) = call(
        side_kernel, "side", far(pops) + kept(post, zin, ypin, ymin, nozzle, wall), [shape(19, SX, SZ_, 2 * HALF)],
        [pltpu.VMEM((len(SIDE), SX, SZ_, 2 * HALF), F32), dma((len(SIDE),))], {0: 0},
    )
    return tuple(call(
        final_kernel, "finish",
        far(pops) + kept(post, zin, ypin, ymin, xa, xb, nozzle, wall, temp, cond, cell, edge),
        [shape(19, SX, SZ_, 2 * HALF), shape(SX, DEPTH, HALF)],
        [pltpu.VMEM((X_ROWS, HALF), F32), pltpu.VMEM((X_ROWS, HALF), F32),
         pltpu.VMEM((10, SZ_, 2 * HALF), F32), pltpu.VMEM((SX, DEPTH, HALF), F32), dma((14,))], {0: 0},
    ))


def solution(mesh):
    placed = (
        P(None, "gx", "gz", "gy"),
        P("gx", "gy"),
        P("gx", "gy"),
        P("gx", None, ("gy", "gz")),
        P("gx", None, ("gy", "gz")),
        P("gx", ("gy", "gz")),
        P("gx", ("gy", "gz")),
    )
    return jax.shard_map(
        body,
        mesh=mesh,
        in_specs=placed,
        out_specs=(P(None, "gx", "gz", "gy"), P("gx", None, ("gy", "gz"))),
        check_vma=False,
    )
```
